32 devices in a mesh: energy: 4 (over y, x), domain: 8 (over z, core).
Axes of the slice: x: 2, y: 2, z: 4, core: 2. Of those that a mesh axis runs over, the one named last changes fastest.
Arguments:
- retarded: bfloat16 [4, 16, 256, 512], P('energy', 'domain'), may hold values from -1 to 2
- coupling: bfloat16 [16, 256, 512], P('domain'), may hold values from -1 to 2
- sigma_lesser: bfloat16 [4, 16, 256, 512], P('energy', 'domain'), may hold values from -4 to 4
- sigma_greater: bfloat16 [4, 16, 256, 512], P('energy', 'domain'), may hold values from -4 to 4
- tiles: int32 [16, 2], P('domain'), may hold values from 0 to 3, all different within a row
- offsets: int32 [4], replicated, may hold values from -2 to 2, as said below
Outputs:
- polarization: bfloat16 [4, 16, 2, 128, 256], P('energy', 'domain')
The draws below stay inside these ranges and needn't reach their ends.
Inputs may be any that keep to these rules, and one draw needn't show every extreme that they name: Each row names 2 different tiles. `offsets`: both ends of the range occur in every draw.
All inputs are finite; a program needn't handle non-finite values.
Results may differ from the reference program's by a relative error of at most 0.039.
Values may be sent and summed in bfloat16 or wider, within the bound.
No kernel may reach another device: no remote copies, remote signals or barrier semaphores. Data moves between devices by JAX's collectives and lax.ppermute only.
A program may use at most 64 MiB of HBM per device.

```python
import jax
import jax.numpy as jnp
from jax import lax

B = 256
TILES = 4
TSEL = 2
NE = 4
TRANSPORT_BLOCKS = 16


energy_spread = 0.2


def draw_retarded(key, part):
    rate_key = jax.random.fold_in(key, 11)
    pulse_random_key = jax.random.fold_in(key, 12)
    jitter_key = jax.random.fold_in(key, 13)
    lowest = jnp.log(0.5 / TRANSPORT_BLOCKS)
    highest = jnp.log(0.08)
    decay_losses = jnp.exp(jax.random.uniform(rate_key, (NE,), jnp.float32, lowest, highest))
    tile_positions = jax.random.randint(pulse_random_key, (3,), 0, TRANSPORT_BLOCKS)
    selected_hits = jnp.any(jnp.arange(TRANSPORT_BLOCKS)[:, None] == tile_positions[None, :], axis=1)
    pulse_events = jnp.where(selected_hits, jnp.sqrt(0.6), 1.0)
    scale_factors = jnp.exp(-energy_spread * energy_spread - 0.5 * decay_losses)[:, None] * pulse_events[None, :]
    jitter = jax.random.truncated_normal(jitter_key, -4.0, 4.0, (NE, TRANSPORT_BLOCKS, B, 2 * B), jnp.float32)
    eye_block = jnp.concatenate([jnp.eye(B, dtype=jnp.float32), jnp.zeros((B, B), jnp.float32)], axis=1)
    return (scale_factors[:, :, None, None] * (eye_block + energy_spread * jitter / jnp.sqrt(2.0 * B))).astype(jnp.bfloat16)


def draw_coupling(key, part):
    jitter_key = jax.random.fold_in(key, 21)
    jitter = jax.random.truncated_normal(jitter_key, -4.0, 4.0, (TRANSPORT_BLOCKS, B, 2 * B), jnp.float32)
    eye_block = jnp.concatenate([jnp.eye(B, dtype=jnp.float32), jnp.zeros((B, B), jnp.float32)], axis=1)
    return (eye_block + energy_spread * jitter / jnp.sqrt(2.0 * B)).astype(jnp.bfloat16)


def draw_offsets(key, part):
    value_key = jax.random.fold_in(key, 31)
    place_key = jax.random.fold_in(key, 32)
    lowest_offset = 0 - NE // 2
    highest_offset = NE // 2
    values = jax.random.randint(value_key, (NE,), lowest_offset, highest_offset + 1, jnp.int32)
    places = jax.random.permutation(place_key, NE)
    values = values.at[places[0]].set(lowest_offset)
    values = values.at[places[1]].set(highest_offset)
    return values.astype(jnp.int32)


def levels(own_key, dims, shards, smallest, largest):
    factor_of, own = 1.0, jax.random.fold_in(own_key, 6)
    for axis_at, parts in shards:
        steps = jnp.exp(jax.random.uniform(jax.random.fold_in(own, axis_at), (parts,), jnp.float32, smallest / len(shards), largest / len(shards)))
        factor_of = factor_of * jnp.repeat(steps, dims[axis_at] // parts).reshape([-1 if axis == axis_at else 1 for axis in range(len(dims))])
    return factor_of


def picks_of(own_key, rows, number_of, top, lift):
    order = jax.random.permutation(jax.random.fold_in(own_key, 1), number_of)
    boost = order
    for power in range(3):
        boost = boost * boost // number_of
    boost = boost * lift // number_of
    tickets = jax.random.randint(jax.random.fold_in(own_key, 2), (rows, number_of), 0, 4096) + boost
    holders = jax.random.permutation(jax.random.fold_in(own_key, 3), rows)[jnp.arange(number_of) % rows]
    tickets = jnp.where(jnp.arange(rows)[:, None] == holders[None, :], 1 << 14, tickets)
    score = tickets * number_of + jnp.arange(number_of)
    return lax.top_k(score.astype(jnp.int32), top)[1].astype(jnp.int32)


def centred(rng, extent, spread, reach, split=(), kind=jnp.bfloat16):
    array = jax.random.normal(rng, extent, jnp.float32) * spread
    if len(split) > 0:
        array = levels(rng, extent, split, -0.22, 0.18) * array
    return jnp.clip(array, min=-reach, max=reach).astype(kind)


def setup_inputs(seed: int = 0) -> dict:
    arg_keys = jax.random.split(jax.random.key(seed), 7)
    retarded = draw_retarded(jax.random.fold_in(arg_keys[6], 71), 0)
    coupling = draw_coupling(jax.random.fold_in(arg_keys[6], 71), 0)
    sigma_lesser = centred(arg_keys[2], (NE, TRANSPORT_BLOCKS, B, 2 * B), 0.5, 4.0, ((0, 4), (1, 8)))
    sigma_greater = centred(arg_keys[3], (NE, TRANSPORT_BLOCKS, B, 2 * B), 0.5, 4.0, ((0, 4), (1, 8)))
    tiles = picks_of(arg_keys[4], TRANSPORT_BLOCKS, TILES, TSEL, 0)
    offsets = draw_offsets(jax.random.fold_in(arg_keys[6], 71), 0)
    return dict(retarded=retarded, coupling=coupling, sigma_lesser=sigma_lesser, sigma_greater=sigma_greater, tiles=tiles, offsets=offsets)


def stacked(block):
    block_order = block.shape[-2]
    real_part = block[..., :block_order]
    imag_part = block[..., block_order:]
    bottom = jnp.concatenate([-imag_part, real_part], axis=-1)
    return jnp.concatenate([block, bottom], axis=-2)


def product(factor, second):
    return jnp.matmul(factor.astype(jnp.float32), stacked(second).astype(jnp.float32))


def product_adjoint(factor, second):
    return jnp.matmul(factor.astype(jnp.float32), jnp.swapaxes(stacked(second), -1, -2).astype(jnp.float32))


def to_tiles(block, tile_rows):
    leading = block.shape[:-2]
    leading_count = len(leading)
    pieces = block.reshape(leading + (2, tile_rows, 2, 2, tile_rows))
    axes_order = tuple(range(leading_count)) + (leading_count, leading_count + 3, leading_count + 1, leading_count + 2, leading_count + 4)
    return pieces.transpose(axes_order).reshape(leading + (4, tile_rows, 2 * tile_rows))


def convolve(less_tiles, great_tiles, offsets):
    energies = less_tiles.shape[0]
    tile_rows = less_tiles.shape[-1] // 2
    pad_shape = (energies,) + great_tiles.shape[1:]
    padding = jnp.zeros(pad_shape, great_tiles.dtype)
    padded = jnp.concatenate([padding, great_tiles, padding], axis=0)

    def one_output(offset):
        begin_at = (energies - offset).astype(jnp.int32)
        shifted = lax.dynamic_slice_in_dim(padded, begin_at, energies, 0).astype(jnp.float32)
        less_real = less_tiles[..., :tile_rows].astype(jnp.float32)
        less_imag = less_tiles[..., tile_rows:].astype(jnp.float32)
        great_real = shifted[..., :tile_rows]
        great_imag = shifted[..., tile_rows:]
        out_real = jnp.sum(less_real * great_real - less_imag * great_imag, axis=0)
        out_imag = jnp.sum(less_real * great_imag + less_imag * great_real, axis=0)
        return (jnp.concatenate([out_real, out_imag], axis=-1) / energies).astype(jnp.bfloat16)

    return lax.map(one_output, offsets)


def sweep_step(states, inputs):
    lesser, greater = states
    retarded_block, coupling_block, lesser_source, greater_source, chosen = inputs
    propagator = product(retarded_block, coupling_block).astype(jnp.bfloat16)
    injected_less = product_adjoint(product(retarded_block, lesser_source).astype(jnp.bfloat16), retarded_block).astype(jnp.bfloat16)
    injected_great = product_adjoint(product(retarded_block, greater_source).astype(jnp.bfloat16), retarded_block).astype(jnp.bfloat16)
    lesser = (product_adjoint(product(propagator, lesser).astype(jnp.bfloat16), propagator) + injected_less.astype(jnp.float32)).astype(jnp.bfloat16)
    greater = (product_adjoint(product(propagator, greater).astype(jnp.bfloat16), propagator) + injected_great.astype(jnp.float32)).astype(jnp.bfloat16)
    tile_rows = lesser.shape[-2] // 2
    less_tiles = jnp.take(to_tiles(lesser, tile_rows), chosen, axis=1)
    great_tiles = jnp.take(to_tiles(greater, tile_rows), chosen, axis=1)
    return (lesser, greater), (less_tiles, great_tiles)


def reference(retarded, coupling, sigma_lesser, sigma_greater, tiles, offsets):
    empty_state = jnp.zeros((NE, B, 2 * B), jnp.bfloat16)
    inputs = (jnp.swapaxes(retarded, 0, 1), coupling, jnp.swapaxes(sigma_lesser, 0, 1), jnp.swapaxes(sigma_greater, 0, 1), tiles)
    _, (less_tiles, great_tiles) = lax.scan(sweep_step, (empty_state, empty_state), inputs)
    less_tiles = jnp.swapaxes(less_tiles, 0, 1)
    great_tiles = jnp.swapaxes(great_tiles, 0, 1)
    return convolve(less_tiles, great_tiles, offsets)
```

```python
import functools

import jax
import jax.numpy as jnp
from jax import lax
from jax.experimental import pallas as pl
from jax.experimental.pallas import tpu as pltpu
from jax.sharding import PartitionSpec as P


VMEM_LIMIT = 16 << 20
F32 = jnp.float32
BF16 = jnp.bfloat16
VMEM = pl.BlockSpec(memory_space=pltpu.VMEM)
SMEM = pl.BlockSpec(memory_space=pltpu.SMEM)


def stacked(block):
    order = block.shape[0]
    real, imag = block[:, :order], block[:, order:]
    return jnp.concatenate([block, jnp.concatenate([-imag, real], axis=1)], axis=0)


def times(factor, second_stacked):
    return lax.dot_general(
        factor, second_stacked, (((1,), (0,)), ((), ())), preferred_element_type=F32
    )


def times_adjoint(factor, second_stacked):
    return lax.dot_general(
        factor, second_stacked, (((1,), (1,)), ((), ())), preferred_element_type=F32
    )


def advance(state, step, step_stacked, source):
    moved = times(step, stacked(state)).astype(BF16)
    return (times_adjoint(moved, step_stacked) + source.astype(F32)).astype(BF16)


def kernel_call(body, outs, operands, flops, in_specs=None, scratch=(), out_spec=VMEM):
    moved = sum(x.size * x.dtype.itemsize for x in operands)
    moved += sum(functools.reduce(lambda a, b: a * b, o.shape, 1) * 2 for o in outs)
    return pl.pallas_call(
        body,
        out_shape=outs,
        in_specs=in_specs or [VMEM] * len(operands),
        out_specs=[out_spec] * len(outs),
        scratch_shapes=list(scratch),
        compiler_params=pltpu.CompilerParams(vmem_limit_bytes=VMEM_LIMIT),
        cost_estimate=pl.CostEstimate(
            flops=flops, bytes_accessed=moved, transcendentals=0
        ),
    )(*operands)


def local_lesser(blocks, retarded, coupling, sigma, steps, sources, whole, total):
    state = None
    chain = None
    for k in range(blocks):
        r = retarded[0, k]
        step = times(r, stacked(coupling[k])).astype(BF16)
        steps[k] = step
        moved = times(r, stacked(sigma[0, k])).astype(BF16)
        source = times_adjoint(moved, stacked(r)).astype(BF16)
        sources[k] = source
        state = source if state is None else advance(state, step, stacked(step), source)
        chain = step if chain is None else times(step, stacked(chain)).astype(BF16)
    whole[...] = chain
    total[...] = state


def local_greater(blocks, retarded, sigma, steps, sources, total):
    state = None
    for k in range(blocks):
        r = retarded[0, k]
        moved = times(r, stacked(sigma[0, k])).astype(BF16)
        source = times_adjoint(moved, stacked(r)).astype(BF16)
        sources[k] = source
        step = steps[k]
        state = source if state is None else advance(state, step, stacked(step), source)
    total[...] = state


def advance_kernel(state, step, source, out):
    out[...] = advance(state[...], step[...], stacked(step[...]), source[...])


def chain_kernel(later, earlier, out):
    out[...] = times(later[...], stacked(earlier[...])).astype(BF16)


def sum_of(refs):
    total = refs[0][...]
    for ref in refs[1:]:
        total = total + ref[...]
    return total


def finish_kernel(blocks, energies, mine, tiles, *refs):
    arrived, near, lower_step, lower_source, steps, sources = refs[:6]
    pieces = refs[6 : 6 + energies]
    state_ref, held = refs[6 + energies :]
    upper, group = mine[0], mine[1]

    @pl.when(upper == 1)
    def _():
        state_ref[...] = advance(
            arrived[...], lower_step[...], stacked(lower_step[...]), lower_source[...]
        )

    @pl.when(upper == 0)
    def _():
        state_ref[...] = near[...]

    order = state_ref.shape[0]
    half = order // 2
    chosen = tiles.shape[1]
    rows = blocks * chosen * half // energies
    state = state_ref[...]
    for k in range(blocks):
        step = steps[k]
        state = advance(state, step, stacked(step), sources[k])
        held[k] = state
    for k in range(energies):
        first = (group ^ k) * rows
        block = first // (chosen * half)
        slot = (first // half) % chosen
        tile = tiles[block, slot]
        row = pl.multiple_of((tile // 2) * half + first % half, 16)
        column = (tile % 2) * half
        for part in range(2):
            pieces[k][:, part * half : (part + 1) * half] = held[
                block, pl.ds(row, rows), pl.ds(pl.multiple_of(column + part * order, half), half)
            ]


def convolve_kernel(energies, mine, offsets, *refs):
    less, great = refs[:energies], refs[energies : 2 * energies]
    out = refs[2 * energies]
    held_less, held_great = refs[2 * energies + 1 :]
    group = mine[1]
    rows, width = less[0].shape
    half = width // 2
    for k in range(energies):
        held_less[group ^ k] = less[k][...].astype(F32)
        held_great[energies + (group ^ k)] = great[k][...].astype(F32)
        held_great[k] = jnp.zeros((rows, width), F32)
        held_great[2 * energies + k] = jnp.zeros((rows, width), F32)
    chunk = 16
    for start in range(0, rows, chunk):
        at = slice(start, start + chunk)

        def one_output(m, carry):
            real = jnp.zeros((chunk, half), F32)
            imag = jnp.zeros((chunk, half), F32)
            for e in range(energies):
                other = held_great.at[energies + e - offsets[m]]
                lr, li = held_less[e, at, :half], held_less[e, at, half:]
                gr, gi = other[at, :half], other[at, half:]
                real = real + (lr * gr - li * gi)
                imag = imag + (lr * gi + li * gr)
            out[m, at, :half] = (real / energies).astype(BF16)
            out[m, at, half:] = (imag / energies).astype(BF16)
            return carry

        for m in range(energies):
            one_output(m, 0)


def shards(retarded, coupling, sigma_lesser, sigma_greater, tiles, offsets):
    blocks, order = retarded.shape[1], retarded.shape[2]
    half = order // 2
    chosen = tiles.shape[1]
    domains, energies = lax.axis_size("domain"), lax.axis_size("energy")
    chips = domains // 2
    rows = blocks * chosen * half // energies
    unit = 8 * order**3
    block = jax.ShapeDtypeStruct((order, 2 * order), BF16)
    series = jax.ShapeDtypeStruct((blocks, order, 2 * order), BF16)
    mine = jnp.stack(
        [lax.axis_index("domain") % 2, lax.axis_index("energy")]
    ).astype(jnp.int32)

    def up(x):
        return lax.ppermute(x, "domain", [(2 * z, 2 * z + 1) for z in range(chips)])

    def down(x):
        return lax.ppermute(x, "domain", [(2 * z + 1, 2 * z) for z in range(chips)])

    def hop(x, z):
        return lax.ppermute(x, "domain", [(2 * z - 1, 2 * z + 1)])

    def across(x, k):
        return lax.ppermute(x, "energy", [(e, e ^ k) for e in range(energies)])

    def finish(arrived, lower_source, sources):
        near = down(arrived)
        piece = jax.ShapeDtypeStruct((rows, order), BF16)
        pieces = kernel_call(
            functools.partial(finish_kernel, blocks, energies),
            [piece] * energies,
            (mine, tiles, arrived, near, lower_whole, lower_source, steps, sources),
            2 * (blocks + 1) * unit,
            in_specs=[SMEM] * 2 + [VMEM] * 6,
            scratch=[
                pltpu.VMEM((order, 2 * order), BF16),
                pltpu.VMEM((blocks, order, 2 * order), BF16),
            ],
        )
        return [pieces[0]] + [across(pieces[k], k) for k in range(1, energies)]

    steps, less_sources, whole, less_total = kernel_call(
        functools.partial(local_lesser, blocks),
        [series, series, block, block],
        (retarded, coupling, sigma_lesser),
        9 * unit,
    )
    lower_less = up(less_total)
    great_sources, great_total = kernel_call(
        functools.partial(local_greater, blocks),
        [series, block],
        (retarded, sigma_greater, steps),
        6 * unit,
    )
    lower_great = up(great_total)
    lower_whole = up(whole)

    def step_on(state, step, source):
        return kernel_call(advance_kernel, [block], (state, step, source), 2 * unit)[0]

    chip_less = step_on(lower_less, whole, less_total)
    chip_great = step_on(lower_great, whole, great_total)
    (chip_whole,) = kernel_call(chain_kernel, [block], (whole, lower_whole), unit)
    less, great = chip_less, chip_great
    less_in, great_in = None, None
    for z in range(1, chips):
        less, great = hop(less, z), hop(great, z)
        less_in = less if less_in is None else less_in + less
        great_in = great if great_in is None else great_in + great
        if z < chips - 1:
            less = step_on(less, chip_whole, chip_less)
            great = step_on(great, chip_whole, chip_great)
    less_pieces = finish(less_in, lower_less, less_sources)
    great_pieces = finish(great_in, lower_great, great_sources)
    (shares,) = kernel_call(
        functools.partial(convolve_kernel, energies),
        [jax.ShapeDtypeStruct((energies, rows, order), BF16)],
        (mine, offsets, *less_pieces, *great_pieces),
        8 * energies * energies * rows * half,
        in_specs=[SMEM] * 2 + [VMEM] * (2 * energies),
        scratch=[
            pltpu.VMEM((energies, rows, order), F32),
            pltpu.VMEM((3 * energies, rows, order), F32),
        ],
    )
    result = lax.all_to_all(shares, "energy", split_axis=0, concat_axis=0, tiled=True)
    return result.reshape(1, blocks, chosen, half, order)


def solution(mesh):
    placed = (
        P("energy", "domain", None, None),
        P("domain", None, None),
        P("energy", "domain", None, None),
        P("energy", "domain", None, None),
        P("domain", None),
        P(),
    )
    return jax.shard_map(
        shards,
        mesh=mesh,
        in_specs=placed,
        out_specs=P("energy", "domain", None, None, None),
        check_vma=False,
    )
```

```python
import functools
import math

import jax
import jax.numpy as jnp
from jax import lax
from jax.experimental import pallas as pl
from jax.experimental.pallas import tpu as pltpu
from jax.sharding import PartitionSpec as P


VMEM_LIMIT = 16 << 20
F32 = jnp.float32
BF16 = jnp.bfloat16
VMEM = pl.BlockSpec(memory_space=pltpu.VMEM)
SMEM = pl.BlockSpec(memory_space=pltpu.SMEM)
HBM = pl.BlockSpec(memory_space=pltpu.HBM)


def stacked(block):
    order = block.shape[-1] // 2
    real, imag = block[:, :order], block[:, order:]
    return jnp.concatenate([block, jnp.concatenate([-imag, real], axis=1)], axis=0)


def times(factor, second_stacked):
    return lax.dot_general(
        factor, second_stacked, (((1,), (0,)), ((), ())), preferred_element_type=F32
    )


def times_adjoint(factor, second_stacked):
    return lax.dot_general(
        factor, second_stacked, (((1,), (1,)), ((), ())), preferred_element_type=F32
    )


def product(factor, second):
    return times(factor, stacked(second)).astype(BF16)


def injected(retarded, sigma):
    return times_adjoint(product(retarded, sigma), stacked(retarded)).astype(BF16)


def advance(state, step, source):
    return (times_adjoint(product(step, state), stacked(step)) + source.astype(F32)).astype(
        BF16
    )


def kernel_call(body, outs, operands, flops, in_specs=None, scratch=(), out_specs=None):
    moved = sum(x.size * x.dtype.itemsize for x in operands)
    moved += sum(math.prod(o.shape) * o.dtype.itemsize for o in outs)
    return pl.pallas_call(
        body,
        out_shape=outs,
        in_specs=in_specs or [VMEM] * len(operands),
        out_specs=out_specs or [VMEM] * len(outs),
        scratch_shapes=list(scratch),
        compiler_params=pltpu.CompilerParams(vmem_limit_bytes=VMEM_LIMIT),
        cost_estimate=pl.CostEstimate(
            flops=int(flops), bytes_accessed=moved, transcendentals=0
        ),
    )(*operands)


def first_kernel(
    blocks,
    place,
    tiles,
    offsets,
    retarded,
    coupling,
    lesser,
    greater,
    held_retarded,
    held_coupling,
    held_greater,
    later_steps,
    sources,
    total,
    scalars,
    held_lesser,
    held_tiles,
    held_offsets,
    sem,
):
    copies = {}
    for k in range(blocks):
        copies["r", k] = (retarded.at[0, k], held_retarded.at[k])
        copies["l", k] = (lesser.at[0, k], held_lesser.at[k])
        if k > 0:
            copies["c", k] = (coupling.at[k], held_coupling.at[k])
    copies["c", 0] = (coupling.at[0], held_coupling.at[0])
    for k in range(blocks):
        copies["g", k] = (greater.at[0, k], held_greater.at[k])
    copies["t", 0] = (tiles, held_tiles)
    copies["o", 0] = (offsets, held_offsets)
    for index, key in enumerate(copies):
        copies[key] = pltpu.make_async_copy(*copies[key], sem.at[index])
        copies[key].start()
    state = None
    for k in range(blocks):
        copies["r", k].wait()
        copies["l", k].wait()
        source = injected(held_retarded[k], held_lesser[k])
        sources[k] = source
        if k > 0:
            copies["c", k].wait()
            step = product(held_retarded[k], held_coupling[k])
            later_steps[k - 1] = step
        state = source if k == 0 else advance(state, step, source)
    total[...] = state
    copies["c", 0].wait()
    for k in range(blocks):
        copies["g", k].wait()
    copies["t", 0].wait()
    copies["o", 0].wait()
    chosen = held_tiles.shape[1]
    values = [place[i] for i in range(place.shape[0])]
    values += [held_tiles[k, j] for k in range(blocks) for j in range(chosen)]
    values += [held_offsets[i] for i in range(held_offsets.shape[0])]
    for i, value in enumerate(values):
        scalars[i] = value


def second_kernel(
    blocks, retarded, coupling, greater, later_steps, first_step, sources, totals
):
    state = chain = None
    for k in range(blocks):
        source = injected(retarded[k], greater[k])
        sources[k] = source
        if k == 0:
            chain = product(retarded[0], coupling[0])
            first_step[...] = chain
            state = source
        else:
            step = later_steps[k - 1]
            chain = product(step, chain)
            state = advance(state, step, source)
    totals[0] = state
    totals[1] = chain


def join_lesser_kernel(lower, totals, upper, out):
    out[...] = advance(lower[...], totals[1], upper[...])


def join_greater_kernel(lower, upper, out, whole):
    out[...] = advance(lower[0], upper[1], upper[0])
    whole[...] = product(upper[1], lower[1])


def keep(z, scalars, state, kept, out):
    @pl.when(scalars[1] == z)
    def _():
        out[...] = state[...]

    @pl.when(scalars[1] != z)
    def _():
        out[...] = jnp.zeros_like(out) if kept is None else kept[...]


def advance_kernel(z, scalars, state, step, source, *refs):
    kept, (out, chosen) = (refs[0] if len(refs) == 3 else None), refs[-2:]
    out[...] = advance(state[...], step[...], source[...])
    keep(z, scalars, state, kept, chosen)


def keep_kernel(z, scalars, state, *refs):
    keep(z, scalars, state, refs[0] if len(refs) == 2 else None, refs[-1])


def piece_of(scalars, k, chosen, half, rows):
    first = (scalars[2] ^ k) * rows
    block = first // (chosen * half)
    tile = scalars[3 + first // half]
    return block, tile, first % half


def prepare_kernel(
    blocks,
    energies,
    chosen,
    scalars,
    first_step,
    later_steps,
    lesser_sources,
    greater_sources,
    lower_lesser,
    lower_totals,
    lefts,
    rights,
    lesser_parts,
    greater_parts,
    chains,
    lessers,
    greaters,
):
    order = first_step.shape[0]
    half = order // 2
    rows = blocks * chosen * half // energies

    @pl.when(scalars[0] == 0)
    def _():
        chains[0] = first_step[...]
        lessers[0] = lesser_sources[0]
        greaters[0] = greater_sources[0]

    @pl.when(scalars[0] == 1)
    def _():
        chains[0] = product(first_step[...], lower_totals[1])
        lessers[0] = advance(lower_lesser[...], first_step[...], lesser_sources[0])
        greaters[0] = advance(lower_totals[0], first_step[...], greater_sources[0])

    for k in range(1, blocks):
        step = later_steps[k - 1]
        chains[k] = product(step, chains[k - 1])
        lessers[k] = advance(lessers[k - 1], step, lesser_sources[k])
        greaters[k] = advance(greaters[k - 1], step, greater_sources[k])
    for k in range(energies):
        block, tile, start = piece_of(scalars, k, chosen, half, rows)
        row = pl.multiple_of((tile // 2) * half + start, 16)
        column = pl.multiple_of((tile % 2) * half, half)
        mine = slice(k * rows, (k + 1) * rows)
        lefts[mine] = chains[block, pl.ds(row, rows), :]
        rights[k] = stacked(chains[block, pl.ds(column, half), :])
        for whole, parts in ((lessers, lesser_parts), (greaters, greater_parts)):
            for part in range(2):
                at = pl.ds(pl.multiple_of(column + part * order, half), half)
                parts[mine, part * half : (part + 1) * half] = whole[
                    block, pl.ds(row, rows), at
                ]


def finish_kernel(energies, scalars, arrived, near, lefts, rights, parts, *refs):
    pieces, doubled = refs[:energies], refs[energies]
    rows = parts.shape[0] // energies

    @pl.when(scalars[0] == 1)
    def _():
        doubled[...] = stacked(arrived[...])

    @pl.when(scalars[0] == 0)
    def _():
        doubled[...] = stacked(near[...])

    moved = times(lefts[...], doubled[...]).astype(BF16)
    for k in range(energies):
        mine = slice(k * rows, (k + 1) * rows)
        pieces[k][...] = (
            times_adjoint(moved[mine], rights[k]) + parts[mine].astype(F32)
        ).astype(BF16)


def convolve_kernel(energies, at_offsets, scalars, *refs):
    less, great = refs[:energies], refs[energies : 2 * energies]
    outs = refs[2 * energies : 3 * energies]
    held_less, held_great = refs[3 * energies :]
    group = scalars[2]
    rows, width = less[0].shape
    half = width // 2
    for k in range(energies):
        held_less[group ^ k] = less[k][...].astype(F32)
        held_great[energies + (group ^ k)] = great[k][...].astype(F32)
        held_great[k] = jnp.zeros((rows, width), F32)
        held_great[2 * energies + k] = jnp.zeros((rows, width), F32)
    chunk = 16
    for start in range(0, rows, chunk):
        at = slice(start, start + chunk)
        for k in range(energies):
            shift = energies - scalars[at_offsets + (group ^ k)]
            real = jnp.zeros((chunk, half), F32)
            imag = jnp.zeros((chunk, half), F32)
            for e in range(energies):
                other = held_great.at[shift + e]
                lr, li = held_less[e, at, :half], held_less[e, at, half:]
                gr, gi = other[at, :half], other[at, half:]
                real = real + (lr * gr - li * gi)
                imag = imag + (lr * gi + li * gr)
            outs[k][at, :half] = (real / energies).astype(BF16)
            outs[k][at, half:] = (imag / energies).astype(BF16)


def gather_kernel(energies, scalars, *refs):
    shares, (out, sem) = refs[:energies], refs[energies:]
    copies = [
        pltpu.make_async_copy(shares[k], out.at[scalars[2] ^ k], sem.at[k])
        for k in range(energies)
    ]
    for copy in copies:
        copy.start()
    for copy in copies:
        copy.wait()


def shards(retarded, coupling, sigma_lesser, sigma_greater, tiles, offsets):
    blocks, order = retarded.shape[1], retarded.shape[2]
    half = order // 2
    chosen = tiles.shape[1]
    domains, energies = lax.axis_size("domain"), lax.axis_size("energy")
    chips = domains // 2
    rows = blocks * chosen * half // energies
    unit = 8 * order**3
    block = jax.ShapeDtypeStruct((order, 2 * order), BF16)
    piece = jax.ShapeDtypeStruct((rows, order), BF16)

    def series(count):
        return jax.ShapeDtypeStruct((count, order, 2 * order), BF16)

    domain = lax.axis_index("domain")
    place = jnp.stack([domain & 1, domain >> 1, lax.axis_index("energy")])
    at_offsets = place.size + tiles.size

    def swap(x):
        return lax.ppermute(x, "domain", [(d, d ^ 1) for d in range(domains)])

    def hop(x, z):
        last = 2 * z - 1
        ring = [last, last + 2, last + 1, last - 1]
        route = dict(zip(ring, ring[1:] + ring[:1]))
        return lax.ppermute(
            x, "domain", [(d, route.get(d, d ^ 1)) for d in range(domains)]
        )

    def across(x, k):
        return lax.ppermute(x, "energy", [(e, e ^ k) for e in range(energies)])

    inputs = (tiles, offsets, retarded, coupling, sigma_lesser, sigma_greater)
    (
        held_retarded,
        held_coupling,
        held_greater,
        later_steps,
        less_sources,
        less_total,
        scalars,
    ) = kernel_call(
        functools.partial(first_kernel, blocks),
        [series(blocks)] * 3
        + [series(blocks - 1), series(blocks), block]
        + [jax.ShapeDtypeStruct((at_offsets + offsets.size,), jnp.int32)],
        (place,)
        + tuple(pltpu.with_memory_space_constraint(x, pltpu.HBM) for x in inputs),
        (5 * blocks - 3) * unit,
        in_specs=[SMEM] + [HBM] * len(inputs),
        out_specs=[VMEM] * 6 + [SMEM],
        scratch=[
            pltpu.VMEM((blocks, order, 2 * order), BF16),
            pltpu.SMEM(tiles.shape, jnp.int32),
            pltpu.SMEM(offsets.shape, jnp.int32),
            pltpu.SemaphoreType.DMA((4 * blocks + 2,)),
        ],
    )
    lower_less = swap(less_total)
    first_step, great_sources, totals = kernel_call(
        functools.partial(second_kernel, blocks),
        [block, series(blocks), series(2)],
        (held_retarded, held_coupling, held_greater, later_steps),
        (5 * blocks - 2) * unit,
    )
    lower_totals = swap(totals)
    (chip_less,) = kernel_call(
        join_lesser_kernel, [block], (lower_less, totals, less_total), 2 * unit
    )
    chip_great, chip_whole = kernel_call(
        join_greater_kernel, [block] * 2, (lower_totals, totals), 3 * unit
    )
    lefts, rights, less_parts, great_parts = kernel_call(
        functools.partial(prepare_kernel, blocks, energies, chosen),
        [
            jax.ShapeDtypeStruct((energies * rows, 2 * order), BF16),
            jax.ShapeDtypeStruct((energies, order, 2 * order), BF16),
            jax.ShapeDtypeStruct((energies * rows, order), BF16),
            jax.ShapeDtypeStruct((energies * rows, order), BF16),
        ],
        (
            scalars,
            first_step,
            later_steps,
            less_sources,
            great_sources,
            lower_less,
            lower_totals,
        ),
        5 * blocks * unit,
        in_specs=[SMEM] + [VMEM] * 6,
        scratch=[pltpu.VMEM((blocks, order, 2 * order), BF16)] * 3,
    )

    def step_on(z, state, kept, source):
        return kernel_call(
            functools.partial(advance_kernel, z),
            [block, block],
            (scalars, state, chip_whole, source, *kept),
            2 * unit,
            in_specs=[SMEM] + [VMEM] * (3 + len(kept)),
        )

    def keep_last(state, kept):
        return kernel_call(
            functools.partial(keep_kernel, chips - 1),
            [block],
            (scalars, state, *kept),
            0,
            in_specs=[SMEM] + [VMEM] * (1 + len(kept)),
        )

    def finish(arrived, parts):
        near = swap(arrived)
        pieces = kernel_call(
            functools.partial(finish_kernel, energies),
            [piece] * energies,
            (scalars, arrived, near, lefts, rights, parts),
            3 * unit,
            in_specs=[SMEM] + [VMEM] * 5,
            scratch=[pltpu.VMEM((2 * order, 2 * order), BF16)],
        )
        return [pieces[0]] + [across(pieces[k], k) for k in range(1, energies)]

    less, great = chip_less, chip_great
    less_in, great_in = (), ()
    for z in range(1, chips):
        less, great = hop(less, z), hop(great, z)
        if z < chips - 1:
            less, *less_in = step_on(z, less, less_in, chip_less)
            great, *great_in = step_on(z, great, great_in, chip_great)
        else:
            less_in = keep_last(less, less_in)
            great_in = keep_last(great, great_in)
    less_pieces = finish(less_in[0], less_parts)
    great_pieces = finish(great_in[0], great_parts)
    shares = kernel_call(
        functools.partial(convolve_kernel, energies, at_offsets),
        [piece] * energies,
        (scalars, *less_pieces, *great_pieces),
        8 * energies * energies * rows * half,
        in_specs=[SMEM] + [VMEM] * (2 * energies),
        scratch=[
            pltpu.VMEM((energies, rows, order), F32),
            pltpu.VMEM((3 * energies, rows, order), F32),
        ],
    )
    shares = [shares[0]] + [across(shares[k], k) for k in range(1, energies)]
    (result,) = kernel_call(
        functools.partial(gather_kernel, energies),
        [jax.ShapeDtypeStruct((energies, rows, order), BF16)],
        (scalars, *shares),
        0,
        in_specs=[SMEM] + [VMEM] * energies,
        out_specs=[HBM],
        scratch=[pltpu.SemaphoreType.DMA((energies,))],
    )
    return result.reshape(1, blocks, chosen, half, order)


def solution(mesh):
    placed = (
        P("energy", "domain", None, None),
        P("domain", None, None),
        P("energy", "domain", None, None),
        P("energy", "domain", None, None),
        P("domain", None),
        P(),
    )

    return jax.shard_map(
        shards,
        mesh=mesh,
        in_specs=placed,
        out_specs=P("energy", "domain", None, None, None),
        check_vma=False,
    )
```

```python
import functools
import math

import jax
import jax.numpy as jnp
from jax import lax
from jax.experimental import pallas as pl
from jax.experimental.pallas import tpu as pltpu
from jax.sharding import PartitionSpec as P


VMEM_LIMIT = 16 << 20
F32 = jnp.float32
BF16 = jnp.bfloat16
VMEM = pl.BlockSpec(memory_space=pltpu.VMEM)
HBM = pl.BlockSpec(memory_space=pltpu.HBM)


def stacked(block):
    order = block.shape[-1] // 2
    real, imag = block[:, :order], block[:, order:]
    return jnp.concatenate([block, jnp.concatenate([-imag, real], axis=1)], axis=0)


def times(factor, second_stacked):
    return lax.dot_general(
        factor, second_stacked, (((1,), (0,)), ((), ())), preferred_element_type=F32
    )


def times_adjoint(factor, second_stacked):
    return lax.dot_general(
        factor, second_stacked, (((1,), (1,)), ((), ())), preferred_element_type=F32
    )


def product(factor, second):
    return times(factor, stacked(second)).astype(BF16)


def injected(retarded, sigma):
    return times_adjoint(product(retarded, sigma), stacked(retarded)).astype(BF16)


def advance(state, step, source):
    return (times_adjoint(product(step, state), stacked(step)) + source.astype(F32)).astype(
        BF16
    )


def kernel_call(body, outs, operands, flops, in_specs=None, scratch=(), out_specs=None):
    moved = sum(x.size * x.dtype.itemsize for x in operands)
    moved += sum(math.prod(o.shape) * o.dtype.itemsize for o in outs)
    return pl.pallas_call(
        body,
        out_shape=outs,
        in_specs=in_specs or [VMEM] * len(operands),
        out_specs=out_specs or [VMEM] * len(outs),
        scratch_shapes=list(scratch),
        compiler_params=pltpu.CompilerParams(vmem_limit_bytes=VMEM_LIMIT),
        cost_estimate=pl.CostEstimate(
            flops=int(flops), bytes_accessed=moved, transcendentals=0
        ),
    )(*operands)


class Copies:
    def __init__(self, source, target, sems):
        parts = sems.shape[0]
        rows = target.shape[0] // parts
        self.parts = [
            pltpu.make_async_copy(
                source.at[pl.ds(i * rows, rows)], target.at[pl.ds(i * rows, rows)], sems.at[i]
            )
            for i in range(parts)
        ]
        for part in self.parts:
            part.start()

    def wait(self):
        for part in self.parts:
            part.wait()


def first_kernel(
    blocks,
    retarded,
    coupling,
    lesser,
    greater,
    held_retarded,
    held_coupling,
    held_greater,
    later_steps,
    sources,
    total,
    held_lesser,
    sem,
):
    copies = {}
    for k in range(blocks):
        copies["r", k] = (retarded.at[0, k], held_retarded.at[k])
        copies["l", k] = (lesser.at[0, k], held_lesser.at[k])
        if k > 0:
            copies["c", k] = (coupling.at[k], held_coupling.at[k])
    copies["c", 0] = (coupling.at[0], held_coupling.at[0])
    for k in range(blocks):
        copies["g", k] = (greater.at[0, k], held_greater.at[k])
    for index, (key, (source, target)) in enumerate(copies.items()):
        copies[key] = Copies(source, target, sem.at[index])
    state = None
    for k in range(blocks):
        copies["r", k].wait()
        copies["l", k].wait()
        source = injected(held_retarded[k], held_lesser[k])
        sources[k] = source
        if k > 0:
            copies["c", k].wait()
            step = product(held_retarded[k], held_coupling[k])
            later_steps[k - 1] = step
        state = source if k == 0 else advance(state, step, source)
    total[...] = state
    copies["c", 0].wait()
    for k in range(blocks):
        copies["g", k].wait()


def second_kernel(
    blocks, retarded, coupling, greater, later_steps, first_step, sources, totals
):
    state = chain = None
    for k in range(blocks):
        source = injected(retarded[k], greater[k])
        sources[k] = source
        if k == 0:
            chain = product(retarded[0], coupling[0])
            first_step[...] = chain
            state = source
        else:
            step = later_steps[k - 1]
            chain = product(step, chain)
            state = advance(state, step, source)
    totals[0] = state
    totals[1] = chain


def join_lesser_kernel(lower, totals, upper, out):
    out[...] = advance(lower[...], totals[1], upper[...])


def join_greater_kernel(lower, upper, out, whole):
    out[...] = advance(lower[0], upper[1], upper[0])
    whole[...] = product(upper[1], lower[1])


def keep(z, state, kept, out):
    chip = lax.axis_index("domain") >> 1

    @pl.when(chip == z)
    def _():
        out[...] = state[...]

    @pl.when(chip != z)
    def _():
        out[...] = jnp.zeros_like(out) if kept is None else kept[...]


def advance_kernel(z, state, step, source, *refs):
    kept, (out, chosen) = (refs[0] if len(refs) == 3 else None), refs[-2:]
    out[...] = advance(state[...], step[...], source[...])
    keep(z, state, kept, chosen)


def keep_kernel(z, state, *refs):
    keep(z, state, refs[0] if len(refs) == 2 else None, refs[-1])


def prepare_kernel(
    blocks,
    energies,
    chosen,
    tiles,
    offsets,
    first_step,
    later_steps,
    lesser_sources,
    greater_sources,
    lower_lesser,
    lower_totals,
    lefts,
    rights,
    lesser_parts,
    greater_parts,
    shifts,
    chains,
    lessers,
    greaters,
    held_tiles,
    held_offsets,
    sem,
):
    copies = [
        pltpu.make_async_copy(tiles, held_tiles, sem.at[0]),
        pltpu.make_async_copy(offsets, held_offsets, sem.at[1]),
    ]
    for copy in copies:
        copy.start()
    upper = lax.axis_index("domain") & 1
    group = lax.axis_index("energy")
    order = first_step.shape[0]
    half = order // 2
    rows = blocks * chosen * half // energies

    @pl.when(upper == 0)
    def _():
        chains[0] = first_step[...]
        lessers[0] = lesser_sources[0]
        greaters[0] = greater_sources[0]

    @pl.when(upper == 1)
    def _():
        chains[0] = product(first_step[...], lower_totals[1])
        lessers[0] = advance(lower_lesser[...], first_step[...], lesser_sources[0])
        greaters[0] = advance(lower_totals[0], first_step[...], greater_sources[0])

    for k in range(1, blocks):
        step = later_steps[k - 1]
        chains[k] = product(step, chains[k - 1])
        lessers[k] = advance(lessers[k - 1], step, lesser_sources[k])
        greaters[k] = advance(greaters[k - 1], step, greater_sources[k])
    for copy in copies:
        copy.wait()
    for k in range(energies):
        shifts[k] = jnp.full(shifts.shape[1:], held_offsets[group ^ k], jnp.int32)
        first = (group ^ k) * rows
        block = first // (chosen * half)
        tile = held_tiles[block, (first // half) % chosen]
        start = first % half
        row = pl.multiple_of((tile // 2) * half + start, 16)
        column = pl.multiple_of((tile % 2) * half, half)
        mine = slice(k * rows, (k + 1) * rows)
        lefts[mine] = chains[block, pl.ds(row, rows), :]
        rights[k] = stacked(chains[block, pl.ds(column, half), :])
        for whole, parts in ((lessers, lesser_parts), (greaters, greater_parts)):
            for part in range(2):
                at = pl.ds(pl.multiple_of(column + part * order, half), half)
                parts[mine, part * half : (part + 1) * half] = whole[
                    block, pl.ds(row, rows), at
                ]


def finish_kernel(energies, arrived, near, lefts, rights, parts, *refs):
    pieces, doubled = refs[:energies], refs[energies]
    rows = parts.shape[0] // energies
    upper = lax.axis_index("domain") & 1

    @pl.when(upper == 1)
    def _():
        doubled[...] = stacked(arrived[...])

    @pl.when(upper == 0)
    def _():
        doubled[...] = stacked(near[...])

    moved = times(lefts[...], doubled[...]).astype(BF16)
    for k in range(energies):
        mine = slice(k * rows, (k + 1) * rows)
        pieces[k][...] = (
            times_adjoint(moved[mine], rights[k]) + parts[mine].astype(F32)
        ).astype(BF16)


def convolve_kernel(energies, shifts, *refs):
    less, great = refs[:energies], refs[energies : 2 * energies]
    outs = refs[2 * energies : 3 * energies]
    held_less, held_great = refs[3 * energies :]
    group = lax.axis_index("energy")
    rows, width = less[0].shape
    half = width // 2
    reach = energies // 2
    for k in range(energies):
        held_less[group ^ k] = less[k][...]
        held_great[group ^ k] = great[k][...]
    chunk = 16
    for start in range(0, rows, chunk):
        at = slice(start, start + chunk)
        totals = [None] * energies
        wanted = [jnp.broadcast_to(shifts[k, :1], (chunk, half)) for k in range(energies)]
        for distance in range(-reach, reach + 1):
            real = imag = None
            for e in range(max(0, distance), min(energies, energies + distance)):
                lr = held_less[e, at, :half].astype(F32)
                li = held_less[e, at, half:].astype(F32)
                gr = held_great[e - distance, at, :half].astype(F32)
                gi = held_great[e - distance, at, half:].astype(F32)
                more_real, more_imag = lr * gr - li * gi, lr * gi + li * gr
                real = more_real if real is None else real + more_real
                imag = more_imag if imag is None else imag + more_imag
            for k in range(energies):
                if totals[k] is None:
                    totals[k] = (real, imag)
                else:
                    match = wanted[k] == distance
                    totals[k] = (
                        jnp.where(match, real, totals[k][0]),
                        jnp.where(match, imag, totals[k][1]),
                    )
        for k in range(energies):
            outs[k][at, :half] = (totals[k][0] / energies).astype(BF16)
            outs[k][at, half:] = (totals[k][1] / energies).astype(BF16)


def gather_kernel(energies, *refs):
    shares, (out, sem) = refs[:energies], refs[energies:]
    group = lax.axis_index("energy")
    copies = [
        pltpu.make_async_copy(shares[k], out.at[group ^ k], sem.at[k])
        for k in range(energies)
    ]
    for copy in copies:
        copy.start()
    for copy in copies:
        copy.wait()


def shards(retarded, coupling, sigma_lesser, sigma_greater, tiles, offsets):
    blocks, order = retarded.shape[1], retarded.shape[2]
    half = order // 2
    chosen = tiles.shape[1]
    domains, energies = lax.axis_size("domain"), lax.axis_size("energy")
    chips = domains // 2
    rows = blocks * chosen * half // energies
    unit = 8 * order**3
    block = jax.ShapeDtypeStruct((order, 2 * order), BF16)
    piece = jax.ShapeDtypeStruct((rows, order), BF16)

    def series(count):
        return jax.ShapeDtypeStruct((count, order, 2 * order), BF16)

    def in_place(*arrays):
        return tuple(pltpu.with_memory_space_constraint(x, pltpu.HBM) for x in arrays)

    def swap(x):
        return lax.ppermute(x, "domain", [(d, d ^ 1) for d in range(domains)])

    def hop(x, z):
        last = 2 * z - 1
        ring = [last, last + 2, last + 1, last - 1]
        route = dict(zip(ring, ring[1:] + ring[:1]))
        return lax.ppermute(
            x, "domain", [(d, route.get(d, d ^ 1)) for d in range(domains)]
        )

    def across(x, k):
        return lax.ppermute(x, "energy", [(e, e ^ k) for e in range(energies)])

    held_retarded, held_coupling, held_greater, later_steps, less_sources, less_total = (
        kernel_call(
            functools.partial(first_kernel, blocks),
            [series(blocks)] * 3 + [series(blocks - 1), series(blocks), block],
            in_place(retarded, coupling, sigma_lesser, sigma_greater),
            (5 * blocks - 3) * unit,
            in_specs=[HBM] * 4,
            scratch=[
                pltpu.VMEM((blocks, order, 2 * order), BF16),
                pltpu.SemaphoreType.DMA((4 * blocks, 2)),
            ],
        )
    )
    lower_less = swap(less_total)
    first_step, great_sources, totals = kernel_call(
        functools.partial(second_kernel, blocks),
        [block, series(blocks), series(2)],
        (held_retarded, held_coupling, held_greater, later_steps),
        (5 * blocks - 2) * unit,
    )
    lower_totals = swap(totals)
    (chip_less,) = kernel_call(
        join_lesser_kernel, [block], (lower_less, totals, less_total), 2 * unit
    )
    chip_great, chip_whole = kernel_call(
        join_greater_kernel, [block] * 2, (lower_totals, totals), 3 * unit
    )
    lefts, rights, less_parts, great_parts, shifts = kernel_call(
        functools.partial(prepare_kernel, blocks, energies, chosen),
        [
            jax.ShapeDtypeStruct((energies * rows, 2 * order), BF16),
            jax.ShapeDtypeStruct((energies, order, 2 * order), BF16),
            jax.ShapeDtypeStruct((energies * rows, order), BF16),
            jax.ShapeDtypeStruct((energies * rows, order), BF16),
            jax.ShapeDtypeStruct((energies, 8, half), jnp.int32),
        ],
        (
            *in_place(tiles, offsets),
            first_step,
            later_steps,
            less_sources,
            great_sources,
            lower_less,
            lower_totals,
        ),
        5 * blocks * unit,
        in_specs=[HBM] * 2 + [VMEM] * 6,
        scratch=[pltpu.VMEM((blocks, order, 2 * order), BF16)] * 3
        + [
            pltpu.SMEM(tiles.shape, jnp.int32),
            pltpu.SMEM(offsets.shape, jnp.int32),
            pltpu.SemaphoreType.DMA((2,)),
        ],
    )

    def step_on(z, state, kept, source):
        return kernel_call(
            functools.partial(advance_kernel, z),
            [block, block],
            (state, chip_whole, source, *kept),
            2 * unit,
        )

    def keep_last(state, kept):
        return kernel_call(
            functools.partial(keep_kernel, chips - 1), [block], (state, *kept), 0
        )

    def finish(arrived, parts):
        near = swap(arrived)
        pieces = kernel_call(
            functools.partial(finish_kernel, energies),
            [piece] * energies,
            (arrived, near, lefts, rights, parts),
            3 * unit,
            scratch=[pltpu.VMEM((2 * order, 2 * order), BF16)],
        )
        return [pieces[0]] + [across(pieces[k], k) for k in range(1, energies)]

    less, great = chip_less, chip_great
    less_in, great_in = (), ()
    for z in range(1, chips):
        less, great = hop(less, z), hop(great, z)
        if z < chips - 1:
            less, *less_in = step_on(z, less, less_in, chip_less)
            great, *great_in = step_on(z, great, great_in, chip_great)
        else:
            less_in = keep_last(less, less_in)
            great_in = keep_last(great, great_in)
    less_pieces = finish(less_in[0], less_parts)
    great_pieces = finish(great_in[0], great_parts)
    shares = kernel_call(
        functools.partial(convolve_kernel, energies),
        [piece] * energies,
        (shifts, *less_pieces, *great_pieces),
        8 * energies * energies * rows * half,
        scratch=[pltpu.VMEM((energies, rows, order), BF16)] * 2,
    )
    shares = [shares[0]] + [across(shares[k], k) for k in range(1, energies)]
    (result,) = kernel_call(
        functools.partial(gather_kernel, energies),
        [jax.ShapeDtypeStruct((energies, rows, order), BF16)],
        shares,
        0,
        out_specs=[HBM],
        scratch=[pltpu.SemaphoreType.DMA((energies,))],
    )
    return result.reshape(1, blocks, chosen, half, order)


def solution(mesh):
    placed = (
        P("energy", "domain", None, None),
        P("domain", None, None),
        P("energy", "domain", None, None),
        P("energy", "domain", None, None),
        P("domain", None),
        P(),
    )

    return jax.shard_map(
        shards,
        mesh=mesh,
        in_specs=placed,
        out_specs=P("energy", "domain", None, None, None),
        check_vma=False,
    )
```

```python
import functools
import math

import jax
import jax.numpy as jnp
from jax import lax
from jax.experimental import pallas as pl
from jax.experimental.pallas import tpu as pltpu
from jax.sharding import PartitionSpec as P


VMEM_LIMIT = 16 << 20
F32 = jnp.float32
BF16 = jnp.bfloat16
VMEM = pl.BlockSpec(memory_space=pltpu.VMEM)
HBM = pl.BlockSpec(memory_space=pltpu.HBM)


def stacked(block):
    order = block.shape[-1] // 2
    real, imag = block[:, :order], block[:, order:]
    return jnp.concatenate([block, jnp.concatenate([-imag, real], axis=1)], axis=0)


def times(factor, second_stacked):
    return lax.dot_general(
        factor, second_stacked, (((1,), (0,)), ((), ())), preferred_element_type=F32
    )


def times_adjoint(factor, second_stacked):
    return lax.dot_general(
        factor, second_stacked, (((1,), (1,)), ((), ())), preferred_element_type=F32
    )


def product(factor, second):
    return times(factor, stacked(second)).astype(BF16)


def injected(retarded, sigma):
    return times_adjoint(product(retarded, sigma), stacked(retarded)).astype(BF16)


def advance(state, step, source):
    return (times_adjoint(product(step, state), stacked(step)) + source.astype(F32)).astype(
        BF16
    )


def kernel_call(body, outs, operands, flops, in_specs=None, scratch=(), out_specs=None):
    moved = sum(x.size * x.dtype.itemsize for x in operands)
    moved += sum(math.prod(o.shape) * o.dtype.itemsize for o in outs)
    return pl.pallas_call(
        body,
        out_shape=outs,
        in_specs=in_specs or [VMEM] * len(operands),
        out_specs=out_specs or [VMEM] * len(outs),
        scratch_shapes=list(scratch),
        compiler_params=pltpu.CompilerParams(vmem_limit_bytes=VMEM_LIMIT),
        cost_estimate=pl.CostEstimate(
            flops=int(flops), bytes_accessed=moved, transcendentals=0
        ),
    )(*operands)


class Copies:
    def __init__(self, source, target, sems):
        parts = sems.shape[0]
        rows = target.shape[0] // parts
        self.parts = [
            pltpu.make_async_copy(
                source.at[pl.ds(i * rows, rows)], target.at[pl.ds(i * rows, rows)], sems.at[i]
            )
            for i in range(parts)
        ]
        for part in self.parts:
            part.start()

    def wait(self):
        for part in self.parts:
            part.wait()


def first_kernel(
    blocks,
    retarded,
    coupling,
    lesser,
    greater,
    held_retarded,
    held_coupling,
    held_greater,
    later_steps,
    sources,
    total,
    held_lesser,
    sem,
):
    copies = {}
    for k in range(blocks):
        copies["r", k] = (retarded.at[0, k], held_retarded.at[k])
        copies["l", k] = (lesser.at[0, k], held_lesser.at[k])
        if k > 0:
            copies["c", k] = (coupling.at[k], held_coupling.at[k])
    copies["c", 0] = (coupling.at[0], held_coupling.at[0])
    for k in range(blocks):
        copies["g", k] = (greater.at[0, k], held_greater.at[k])
    for index, (key, (source, target)) in enumerate(copies.items()):
        copies[key] = Copies(source, target, sem.at[index])
    state = None
    for k in range(blocks):
        copies["r", k].wait()
        copies["l", k].wait()
        source = injected(held_retarded[k], held_lesser[k])
        sources[k] = source
        if k > 0:
            copies["c", k].wait()
            step = product(held_retarded[k], held_coupling[k])
            later_steps[k - 1] = step
        state = source if k == 0 else advance(state, step, source)
    total[...] = state
    copies["c", 0].wait()
    for k in range(blocks):
        copies["g", k].wait()


def second_kernel(
    blocks, retarded, coupling, greater, later_steps, first_step, sources, total, whole
):
    state = chain = None
    for k in range(blocks):
        source = injected(retarded[k], greater[k])
        sources[k] = source
        if k == 0:
            chain = product(retarded[0], coupling[0])
            first_step[...] = chain
            state = source
        else:
            step = later_steps[k - 1]
            chain = product(step, chain)
            state = advance(state, step, source)
    total[...] = state
    whole[...] = chain


def join_kernel(lower, whole, upper, out):
    out[...] = advance(lower[...], whole[...], upper[...])


def chain_kernel(later, earlier, out):
    out[...] = product(later[...], earlier[...])


def keep(z, state, kept, out):
    chip = lax.axis_index("domain") >> 1

    @pl.when(chip == z)
    def _():
        out[...] = state[...]

    @pl.when(chip != z)
    def _():
        out[...] = jnp.zeros_like(out) if kept is None else kept[...]


def advance_kernel(z, state, step, source, *refs):
    kept, (out, chosen) = (refs[0] if len(refs) == 3 else None), refs[-2:]
    out[...] = advance(state[...], step[...], source[...])
    keep(z, state, kept, chosen)


def keep_kernel(z, state, *refs):
    keep(z, state, refs[0] if len(refs) == 2 else None, refs[-1])


def states_of(blocks, first_step, later_steps, sources, lower, total, chip, states):
    upper = lax.axis_index("domain") & 1

    @pl.when(upper == 0)
    def _():
        states[0] = sources[0]
        if blocks > 1:
            states[blocks - 1] = total[...]

    @pl.when(upper == 1)
    def _():
        if blocks > 1:
            states[0] = advance(lower[...], first_step[...], sources[0])
        states[blocks - 1] = chip[...]

    for k in range(1, blocks - 1):
        states[k] = advance(states[k - 1], later_steps[k - 1], sources[k])


def prepare_lesser_kernel(blocks, *refs):
    states_of(blocks, *refs)


def prepare_kernel(
    blocks,
    energies,
    chosen,
    tiles,
    offsets,
    first_step,
    later_steps,
    greater_sources,
    lower_great,
    great_total,
    chip_great,
    lower_whole,
    whole,
    chip_whole,
    lessers,
    lefts,
    rights,
    lesser_parts,
    greater_parts,
    shifts,
    chains,
    greaters,
    held_tiles,
    held_offsets,
    sem,
):
    copies = [
        pltpu.make_async_copy(tiles, held_tiles, sem.at[0]),
        pltpu.make_async_copy(offsets, held_offsets, sem.at[1]),
    ]
    for copy in copies:
        copy.start()
    upper = lax.axis_index("domain") & 1
    group = lax.axis_index("energy")
    order = first_step.shape[0]
    half = order // 2
    rows = blocks * chosen * half // energies
    states_of(
        blocks,
        first_step,
        later_steps,
        greater_sources,
        lower_great,
        great_total,
        chip_great,
        greaters,
    )

    @pl.when(upper == 0)
    def _():
        chains[0] = first_step[...]
        chains[blocks - 1] = whole[...]

    @pl.when(upper == 1)
    def _():
        if blocks > 1:
            chains[0] = product(first_step[...], lower_whole[...])
        chains[blocks - 1] = chip_whole[...]

    for k in range(1, blocks - 1):
        chains[k] = product(later_steps[k - 1], chains[k - 1])
    for copy in copies:
        copy.wait()
    for k in range(energies):
        shifts[k] = jnp.full(shifts.shape[1:], held_offsets[group ^ k], jnp.int32)
        first = (group ^ k) * rows
        block = first // (chosen * half)
        tile = held_tiles[block, (first // half) % chosen]
        start = first % half
        row = pl.multiple_of((tile // 2) * half + start, 16)
        column = pl.multiple_of((tile % 2) * half, half)
        mine = slice(k * rows, (k + 1) * rows)
        lefts[mine] = chains[block, pl.ds(row, rows), :]
        rights[k] = stacked(chains[block, pl.ds(column, half), :])
        for states, parts in ((lessers, lesser_parts), (greaters, greater_parts)):
            for part in range(2):
                at = pl.ds(pl.multiple_of(column + part * order, half), half)
                parts[mine, part * half : (part + 1) * half] = states[
                    block, pl.ds(row, rows), at
                ]


def finish(energies, arrived, near, lefts, rights, parts, doubled, write):
    rows = parts.shape[0] // energies
    upper = lax.axis_index("domain") & 1

    @pl.when(upper == 1)
    def _():
        doubled[...] = stacked(arrived[...])

    @pl.when(upper == 0)
    def _():
        doubled[...] = stacked(near[...])

    moved = times(lefts[...], doubled[...]).astype(BF16)
    for k in range(energies):
        mine = slice(k * rows, (k + 1) * rows)
        write(
            k,
            (times_adjoint(moved[mine], rights[k]) + parts[mine].astype(F32)).astype(BF16),
        )


def finish_lesser_kernel(energies, arrived, near, lefts, rights, parts, out, doubled):
    def write(k, value):
        out[k] = value

    finish(energies, arrived, near, lefts, rights, parts, doubled, write)


def finish_greater_kernel(energies, arrived, near, lefts, rights, parts, lesser, *refs):
    pieces, doubled = refs[:energies], refs[energies]

    def write(k, value):
        pieces[k][0] = lesser[k]
        pieces[k][1] = value

    finish(energies, arrived, near, lefts, rights, parts, doubled, write)


def convolve_kernel(energies, shifts, *refs):
    pieces, outs = refs[:energies], refs[energies : 2 * energies]
    held_less, held_great = refs[2 * energies :]
    group = lax.axis_index("energy")
    rows, width = outs[0].shape
    half = width // 2
    reach = energies // 2
    for k in range(energies):
        held_less[group ^ k] = pieces[k][0]
        held_great[group ^ k] = pieces[k][1]
    chunk = 16
    for start in range(0, rows, chunk):
        at = slice(start, start + chunk)
        totals = [None] * energies
        wanted = [jnp.broadcast_to(shifts[k, :1], (chunk, half)) for k in range(energies)]
        for distance in range(-reach, reach + 1):
            real = imag = None
            for e in range(max(0, distance), min(energies, energies + distance)):
                lr = held_less[e, at, :half].astype(F32)
                li = held_less[e, at, half:].astype(F32)
                gr = held_great[e - distance, at, :half].astype(F32)
                gi = held_great[e - distance, at, half:].astype(F32)
                more_real, more_imag = lr * gr - li * gi, lr * gi + li * gr
                real = more_real if real is None else real + more_real
                imag = more_imag if imag is None else imag + more_imag
            for k in range(energies):
                if totals[k] is None:
                    totals[k] = (real, imag)
                else:
                    match = wanted[k] == distance
                    totals[k] = (
                        jnp.where(match, real, totals[k][0]),
                        jnp.where(match, imag, totals[k][1]),
                    )
        for k in range(energies):
            outs[k][at, :half] = (totals[k][0] / energies).astype(BF16)
            outs[k][at, half:] = (totals[k][1] / energies).astype(BF16)


def gather_kernel(energies, *refs):
    shares, (out, sem) = refs[:energies], refs[energies:]
    group = lax.axis_index("energy")
    copies = [
        pltpu.make_async_copy(shares[k], out.at[group ^ k], sem.at[k])
        for k in range(energies)
    ]
    for copy in copies:
        copy.start()
    for copy in copies:
        copy.wait()


def shards(retarded, coupling, sigma_lesser, sigma_greater, tiles, offsets):
    blocks, order = retarded.shape[1], retarded.shape[2]
    half = order // 2
    chosen = tiles.shape[1]
    domains, energies = lax.axis_size("domain"), lax.axis_size("energy")
    chips = domains // 2
    rows = blocks * chosen * half // energies
    unit = 8 * order**3
    block = jax.ShapeDtypeStruct((order, 2 * order), BF16)
    piece = jax.ShapeDtypeStruct((rows, order), BF16)

    def series(count):
        return jax.ShapeDtypeStruct((count, order, 2 * order), BF16)

    def in_place(*arrays):
        return tuple(pltpu.with_memory_space_constraint(x, pltpu.HBM) for x in arrays)

    def swap(x):
        return lax.ppermute(x, "domain", [(d, d ^ 1) for d in range(domains)])

    def hop(x, z):
        last = 2 * z - 1
        ring = [last, last + 2, last + 1, last - 1]
        route = dict(zip(ring, ring[1:] + ring[:1]))
        return lax.ppermute(
            x, "domain", [(d, route.get(d, d ^ 1)) for d in range(domains)]
        )

    def across(x, k):
        return lax.ppermute(x, "energy", [(e, e ^ k) for e in range(energies)])

    held_retarded, held_coupling, held_greater, later_steps, less_sources, less_total = (
        kernel_call(
            functools.partial(first_kernel, blocks),
            [series(blocks)] * 3 + [series(blocks - 1), series(blocks), block],
            in_place(retarded, coupling, sigma_lesser, sigma_greater),
            (5 * blocks - 3) * unit,
            in_specs=[HBM] * 4,
            scratch=[
                pltpu.VMEM((blocks, order, 2 * order), BF16),
                pltpu.SemaphoreType.DMA((4 * blocks, 2)),
            ],
        )
    )
    lower_less = swap(less_total)
    first_step, great_sources, great_total, whole = kernel_call(
        functools.partial(second_kernel, blocks),
        [block, series(blocks), block, block],
        (held_retarded, held_coupling, held_greater, later_steps),
        (5 * blocks - 2) * unit,
    )
    lower_great = swap(great_total)
    lower_whole = swap(whole)
    (chip_less,) = kernel_call(
        join_kernel, [block], (lower_less, whole, less_total), 2 * unit
    )
    (chip_great,) = kernel_call(
        join_kernel, [block], (lower_great, whole, great_total), 2 * unit
    )
    (chip_whole,) = kernel_call(chain_kernel, [block], (whole, lower_whole), unit)
    (lessers,) = kernel_call(
        functools.partial(prepare_lesser_kernel, blocks),
        [series(blocks)],
        (first_step, later_steps, less_sources, lower_less, less_total, chip_less),
        2 * unit,
    )
    part = jax.ShapeDtypeStruct((energies * rows, order), BF16)
    lefts, rights, less_parts, great_parts, shifts = kernel_call(
        functools.partial(prepare_kernel, blocks, energies, chosen),
        [
            jax.ShapeDtypeStruct((energies * rows, 2 * order), BF16),
            jax.ShapeDtypeStruct((energies, order, 2 * order), BF16),
            part,
            part,
            jax.ShapeDtypeStruct((energies, 8, half), jnp.int32),
        ],
        (
            *in_place(tiles, offsets),
            first_step,
            later_steps,
            great_sources,
            lower_great,
            great_total,
            chip_great,
            lower_whole,
            whole,
            chip_whole,
            lessers,
        ),
        3 * unit,
        in_specs=[HBM] * 2 + [VMEM] * 10,
        scratch=[pltpu.VMEM((blocks, order, 2 * order), BF16)] * 2
        + [
            pltpu.SMEM(tiles.shape, jnp.int32),
            pltpu.SMEM(offsets.shape, jnp.int32),
            pltpu.SemaphoreType.DMA((2,)),
        ],
    )

    def step_on(z, state, kept, source):
        return kernel_call(
            functools.partial(advance_kernel, z),
            [block, block],
            (state, chip_whole, source, *kept),
            2 * unit,
        )

    def keep_last(state, kept):
        return kernel_call(
            functools.partial(keep_kernel, chips - 1), [block], (state, *kept), 0
        )

    less, great = chip_less, chip_great
    less_in, great_in = (), ()
    for z in range(1, chips):
        less, great = hop(less, z), hop(great, z)
        if z < chips - 1:
            less, *less_in = step_on(z, less, less_in, chip_less)
            great, *great_in = step_on(z, great, great_in, chip_great)
        else:
            less_in = keep_last(less, less_in)
            great_in = keep_last(great, great_in)
    doubled = [pltpu.VMEM((2 * order, 2 * order), BF16)]
    (less_pieces,) = kernel_call(
        functools.partial(finish_lesser_kernel, energies),
        [jax.ShapeDtypeStruct((energies, rows, order), BF16)],
        (*less_in, swap(*less_in), lefts, rights, less_parts),
        3 * unit,
        scratch=doubled,
    )
    pieces = kernel_call(
        functools.partial(finish_greater_kernel, energies),
        [jax.ShapeDtypeStruct((2, rows, order), BF16)] * energies,
        (
            *great_in,
            swap(*great_in),
            lefts,
            rights,
            great_parts,
            less_pieces,
        ),
        3 * unit,
        scratch=doubled,
    )
    pieces = [pieces[0]] + [across(pieces[k], k) for k in range(1, energies)]
    shares = kernel_call(
        functools.partial(convolve_kernel, energies),
        [piece] * energies,
        (shifts, *pieces),
        8 * energies * energies * rows * half,
        scratch=[pltpu.VMEM((energies, rows, order), BF16)] * 2,
    )
    shares = [shares[0]] + [across(shares[k], k) for k in range(1, energies)]
    (result,) = kernel_call(
        functools.partial(gather_kernel, energies),
        [jax.ShapeDtypeStruct((energies, rows, order), BF16)],
        shares,
        0,
        out_specs=[HBM],
        scratch=[pltpu.SemaphoreType.DMA((energies,))],
    )
    return result.reshape(1, blocks, chosen, half, order)


def solution(mesh):
    placed = (
        P("energy", "domain", None, None),
        P("domain", None, None),
        P("energy", "domain", None, None),
        P("energy", "domain", None, None),
        P("domain", None),
        P(),
    )

    return jax.shard_map(
        shards,
        mesh=mesh,
        in_specs=placed,
        out_specs=P("energy", "domain", None, None, None),
        check_vma=False,
    )
```

```python
import functools
import math

import jax
import jax.numpy as jnp
from jax import lax
from jax.experimental import pallas as pl
from jax.experimental.pallas import tpu as pltpu
from jax.sharding import PartitionSpec as P


VMEM_LIMIT = 16 << 20
F32 = jnp.float32
BF16 = jnp.bfloat16
VMEM = pl.BlockSpec(memory_space=pltpu.VMEM)
HBM = pl.BlockSpec(memory_space=pltpu.HBM)


def stacked(block):
    order = block.shape[-1] // 2
    real, imag = block[:, :order], block[:, order:]
    return jnp.concatenate([block, jnp.concatenate([-imag, real], axis=1)], axis=0)


def times(factor, second_stacked):
    return lax.dot_general(
        factor, second_stacked, (((1,), (0,)), ((), ())), preferred_element_type=F32
    )


def times_adjoint(factor, second_stacked):
    return lax.dot_general(
        factor, second_stacked, (((1,), (1,)), ((), ())), preferred_element_type=F32
    )


def product(factor, second):
    return times(factor, stacked(second)).astype(BF16)


def injected(retarded, sigma):
    return times_adjoint(product(retarded, sigma), stacked(retarded)).astype(BF16)


def advance(state, step, source):
    return (times_adjoint(product(step, state), stacked(step)) + source.astype(F32)).astype(
        BF16
    )


def kernel_call(body, outs, operands, flops, in_specs=None, scratch=(), out_specs=None):
    moved = sum(x.size * x.dtype.itemsize for x in operands)
    moved += sum(math.prod(o.shape) * o.dtype.itemsize for o in outs)
    return pl.pallas_call(
        body,
        out_shape=outs,
        in_specs=in_specs or [VMEM] * len(operands),
        out_specs=out_specs or [VMEM] * len(outs),
        scratch_shapes=list(scratch),
        compiler_params=pltpu.CompilerParams(vmem_limit_bytes=VMEM_LIMIT),
        cost_estimate=pl.CostEstimate(
            flops=int(flops), bytes_accessed=moved, transcendentals=0
        ),
    )(*operands)


class Copies:
    def __init__(self, source, target, sems):
        parts = sems.shape[0]
        rows = target.shape[0] // parts
        self.parts = [
            pltpu.make_async_copy(
                source.at[pl.ds(i * rows, rows)], target.at[pl.ds(i * rows, rows)], sems.at[i]
            )
            for i in range(parts)
        ]
        for part in self.parts:
            part.start()

    def wait(self):
        for part in self.parts:
            part.wait()


def first_kernel(
    blocks,
    retarded,
    coupling,
    lesser,
    greater,
    held_retarded,
    held_coupling,
    held_greater,
    later_steps,
    sources,
    total,
    held_lesser,
    sem,
):
    copies = {}
    for k in range(blocks):
        copies["r", k] = (retarded.at[0, k], held_retarded.at[k])
        copies["l", k] = (lesser.at[0, k], held_lesser.at[k])
        if k > 0:
            copies["c", k] = (coupling.at[k], held_coupling.at[k])
    copies["c", 0] = (coupling.at[0], held_coupling.at[0])
    for k in range(blocks):
        copies["g", k] = (greater.at[0, k], held_greater.at[k])
    for index, (key, (source, target)) in enumerate(copies.items()):
        copies[key] = Copies(source, target, sem.at[index])
    state = None
    for k in range(blocks):
        copies["r", k].wait()
        copies["l", k].wait()
        source = injected(held_retarded[k], held_lesser[k])
        sources[k] = source
        if k > 0:
            copies["c", k].wait()
            step = product(held_retarded[k], held_coupling[k])
            later_steps[k - 1] = step
        state = source if k == 0 else advance(state, step, source)
    total[...] = state
    copies["c", 0].wait()
    for k in range(blocks):
        copies["g", k].wait()


def second_kernel(
    blocks, retarded, coupling, greater, later_steps, first_step, sources, total, whole
):
    state = chain = None
    for k in range(blocks):
        source = injected(retarded[k], greater[k])
        sources[k] = source
        if k == 0:
            chain = product(retarded[0], coupling[0])
            first_step[...] = chain
            state = source
        else:
            step = later_steps[k - 1]
            chain = product(step, chain)
            state = advance(state, step, source)
    total[...] = state
    whole[...] = chain


def join_kernel(every_chip, lower, whole, upper, out):
    needed = (lax.axis_index("domain") & 1) == 1
    if not every_chip:
        needed &= (lax.axis_index("domain") >> 1) == 0

    @pl.when(needed)
    def _():
        out[...] = advance(lower[...], whole[...], upper[...])


def chain_kernel(later, earlier, out):
    out[...] = product(later[...], earlier[...])


def keep(z, state, kept, out):
    chip = lax.axis_index("domain") >> 1

    @pl.when(chip == z)
    def _():
        out[...] = state[...]

    @pl.when(chip != z)
    def _():
        out[...] = jnp.zeros_like(out) if kept is None else kept[...]


def advance_kernel(z, state, step, source, *refs):
    kept, (out, chosen) = (refs[0] if len(refs) == 3 else None), refs[-2:]
    out[...] = advance(state[...], step[...], source[...])
    keep(z, state, kept, chosen)


def keep_kernel(z, state, *refs):
    keep(z, state, refs[0] if len(refs) == 2 else None, refs[-1])


def parts_at(energies, rows, half, k):
    below = energies * (rows + half)
    return below + (k // 2) * rows, (k % 2) * 2 * half


def states_of(blocks, first_step, later_steps, sources, lower, total, chip, states):
    upper = lax.axis_index("domain") & 1

    @pl.when(upper == 0)
    def _():
        states[0] = sources[0]
        if blocks > 1:
            states[blocks - 1] = total[...]

    @pl.when(upper == 1)
    def _():
        if blocks > 1:
            states[0] = advance(lower[...], first_step[...], sources[0])
        states[blocks - 1] = chip[...]

    for k in range(1, blocks - 1):
        states[k] = advance(states[k - 1], later_steps[k - 1], sources[k])


def prepare_lesser_kernel(
    blocks,
    whole,
    joined,
    first_step,
    later_steps,
    sources,
    lower,
    total,
    states,
    chip,
):
    first_chip = (lax.axis_index("domain") >> 1) == 0

    @pl.when(first_chip)
    def _():
        chip[...] = joined[...]

    @pl.when(jnp.logical_not(first_chip))
    def _():
        chip[...] = advance(lower[...], whole[...], total[...])

    states_of(blocks, first_step, later_steps, sources, lower, total, chip, states)


def prepare_kernel(
    blocks,
    energies,
    chosen,
    tiles,
    offsets,
    first_step,
    later_steps,
    greater_sources,
    lower_great,
    great_total,
    chip_great,
    lower_whole,
    whole,
    chip_whole,
    lessers,
    given,
    own_parts,
    shifts,
    chains,
    greaters,
    held_tiles,
    held_offsets,
    sem,
):
    copies = [
        pltpu.make_async_copy(tiles, held_tiles, sem.at[0]),
        pltpu.make_async_copy(offsets, held_offsets, sem.at[1]),
    ]
    for copy in copies:
        copy.start()
    upper = lax.axis_index("domain") & 1
    group = lax.axis_index("energy")
    order = first_step.shape[0]
    half = order // 2
    rows = blocks * chosen * half // energies
    states_of(
        blocks,
        first_step,
        later_steps,
        greater_sources,
        lower_great,
        great_total,
        chip_great,
        greaters,
    )

    @pl.when(upper == 0)
    def _():
        chains[0] = first_step[...]
        chains[blocks - 1] = whole[...]

    @pl.when(upper == 1)
    def _():
        if blocks > 1:
            chains[0] = product(first_step[...], lower_whole[...])
        chains[blocks - 1] = chip_whole[...]

    for k in range(1, blocks - 1):
        chains[k] = product(later_steps[k - 1], chains[k - 1])
    for copy in copies:
        copy.wait()
    for k in range(energies):
        shifts[k] = jnp.full(shifts.shape[1:], held_offsets[group ^ k], jnp.int32)
        first = (group ^ k) * rows
        block = first // (chosen * half)
        tile = held_tiles[block, (first // half) % chosen]
        start = first % half
        row = pl.multiple_of((tile // 2) * half + start, 16)
        column = pl.multiple_of((tile % 2) * half, half)
        mine = slice(k * rows, (k + 1) * rows)
        given[mine] = chains[block, pl.ds(row, rows), :]
        others = slice(energies * rows + k * half, energies * rows + (k + 1) * half)
        given[others] = chains[block, pl.ds(column, half), :]

        def pick(states):
            return jnp.concatenate(
                [
                    states[
                        block,
                        pl.ds(row, rows),
                        pl.ds(pl.multiple_of(column + part * order, half), half),
                    ]
                    for part in range(2)
                ],
                axis=1,
            )

        base, side = parts_at(energies, rows, half, k)

        @pl.when(upper == 0)
        def _():
            own_parts[mine] = pick(lessers)
            given[base : base + rows, side : side + order] = pick(greaters)

        @pl.when(upper == 1)
        def _():
            own_parts[mine] = pick(greaters)
            given[base : base + rows, side : side + order] = pick(lessers)


def finish_kernel(energies, lesser, greater, given, taken, own_parts, *refs):
    pieces, doubled = refs[:energies], refs[energies]
    rows, order = pieces[0].shape[1:]
    half = order // 2
    upper = lax.axis_index("domain") & 1

    @pl.when(upper == 0)
    def _():
        doubled[...] = stacked(lesser[...])

    @pl.when(upper == 1)
    def _():
        doubled[...] = stacked(greater[...])

    for source, slot in ((given, upper), (taken, 1 - upper)):
        moved = times(source[: energies * rows], doubled[...]).astype(BF16)
        for k in range(energies):
            first = energies * rows + k * half
            right = stacked(source[first : first + half])
            if source is given:
                part = own_parts[k * rows : (k + 1) * rows]
            else:
                base, side = parts_at(energies, rows, half, k)
                part = source[base : base + rows, side : side + order]
            pieces[k][slot] = (
                times_adjoint(moved[k * rows : (k + 1) * rows], right) + part.astype(F32)
            ).astype(BF16)


def pack_kernel(energies, *refs):
    pieces, out = refs[:energies], refs[energies]
    other = 1 - (lax.axis_index("domain") & 1)
    for k in range(energies):
        out[k] = pieces[k][other]


def convolve_kernel(energies, shifts, swapped, *refs):
    pieces, outs = refs[:energies], refs[energies : 2 * energies]
    upper = lax.axis_index("domain") & 1
    held_less, held_great = refs[2 * energies :]
    group = lax.axis_index("energy")
    rows, width = outs[0].shape
    half = width // 2
    reach = energies // 2

    @pl.when(upper == 0)
    def _():
        for k in range(energies):
            held_less[group ^ k] = pieces[k][0]
            held_great[group ^ k] = swapped[k]

    @pl.when(upper == 1)
    def _():
        for k in range(energies):
            held_less[group ^ k] = swapped[k]
            held_great[group ^ k] = pieces[k][1]

    chunk = 16
    for start in range(0, rows, chunk):
        at = slice(start, start + chunk)
        totals = [None] * energies
        wanted = [jnp.broadcast_to(shifts[k, :1], (chunk, half)) for k in range(energies)]
        for distance in range(-reach, reach + 1):
            real = imag = None
            for e in range(max(0, distance), min(energies, energies + distance)):
                lr = held_less[e, at, :half].astype(F32)
                li = held_less[e, at, half:].astype(F32)
                gr = held_great[e - distance, at, :half].astype(F32)
                gi = held_great[e - distance, at, half:].astype(F32)
                more_real, more_imag = lr * gr - li * gi, lr * gi + li * gr
                real = more_real if real is None else real + more_real
                imag = more_imag if imag is None else imag + more_imag
            for k in range(energies):
                if totals[k] is None:
                    totals[k] = (real, imag)
                else:
                    match = wanted[k] == distance
                    totals[k] = (
                        jnp.where(match, real, totals[k][0]),
                        jnp.where(match, imag, totals[k][1]),
                    )
        for k in range(energies):
            outs[k][at, :half] = (totals[k][0] / energies).astype(BF16)
            outs[k][at, half:] = (totals[k][1] / energies).astype(BF16)


def gather_kernel(energies, *refs):
    shares, (out, sem) = refs[:energies], refs[energies:]
    group = lax.axis_index("energy")
    copies = [
        pltpu.make_async_copy(shares[k], out.at[group ^ k], sem.at[k])
        for k in range(energies)
    ]
    for copy in copies:
        copy.start()
    for copy in copies:
        copy.wait()


def shards(retarded, coupling, sigma_lesser, sigma_greater, tiles, offsets):
    blocks, order = retarded.shape[1], retarded.shape[2]
    half = order // 2
    chosen = tiles.shape[1]
    domains, energies = lax.axis_size("domain"), lax.axis_size("energy")
    chips = domains // 2
    rows = blocks * chosen * half // energies
    unit = 8 * order**3
    block = jax.ShapeDtypeStruct((order, 2 * order), BF16)
    piece = jax.ShapeDtypeStruct((rows, order), BF16)

    def series(count):
        return jax.ShapeDtypeStruct((count, order, 2 * order), BF16)

    def in_place(*arrays):
        return tuple(pltpu.with_memory_space_constraint(x, pltpu.HBM) for x in arrays)

    def swap(x):
        return lax.ppermute(x, "domain", [(d, d ^ 1) for d in range(domains)])

    def hop(x, z):
        last = 2 * z - 1
        if z < chips - 1 or energies % 2:
            ring = [last, last + 2, last + 1, last - 1]
        else:
            ring = [last, last + 2, last - 1]
        onward = dict(zip(ring, ring[1:] + ring[:1]))
        route = []
        for e in range(energies):
            for d in range(domains):
                if d in onward:
                    target = (e, onward[d])
                elif d == last + 1:
                    target = (e ^ 1, d)
                else:
                    target = (e, d ^ 1)
                route.append((e * domains + d, target[0] * domains + target[1]))
        return lax.ppermute(x, ("energy", "domain"), route)

    def across(x, k):
        return lax.ppermute(x, "energy", [(e, e ^ k) for e in range(energies)])

    held_retarded, held_coupling, held_greater, later_steps, less_sources, less_total = (
        kernel_call(
            functools.partial(first_kernel, blocks),
            [series(blocks)] * 3 + [series(blocks - 1), series(blocks), block],
            in_place(retarded, coupling, sigma_lesser, sigma_greater),
            (5 * blocks - 3) * unit,
            in_specs=[HBM] * 4,
            scratch=[
                pltpu.VMEM((blocks, order, 2 * order), BF16),
                pltpu.SemaphoreType.DMA((4 * blocks, 2)),
            ],
        )
    )
    lower_less = swap(less_total)
    first_step, great_sources, great_total, whole = kernel_call(
        functools.partial(second_kernel, blocks),
        [block, series(blocks), block, block],
        (held_retarded, held_coupling, held_greater, later_steps),
        (5 * blocks - 2) * unit,
    )
    lower_great = swap(great_total)
    lower_whole = swap(whole)
    (joined_less,) = kernel_call(
        functools.partial(join_kernel, False),
        [block],
        (lower_less, whole, less_total),
        2 * unit,
    )
    (chip_great,) = kernel_call(
        functools.partial(join_kernel, True),
        [block],
        (lower_great, whole, great_total),
        2 * unit,
    )
    (chip_whole,) = kernel_call(chain_kernel, [block], (whole, lower_whole), unit)
    lessers, chip_less = kernel_call(
        functools.partial(prepare_lesser_kernel, blocks),
        [series(blocks), block],
        (whole, joined_less, first_step, later_steps, less_sources, lower_less, less_total),
        4 * unit,
    )
    given, own_parts, shifts = kernel_call(
        functools.partial(prepare_kernel, blocks, energies, chosen),
        [
            jax.ShapeDtypeStruct(
                (energies * (rows + half) + pl.cdiv(energies, 2) * rows, 2 * order), BF16
            ),
            jax.ShapeDtypeStruct((energies * rows, order), BF16),
            jax.ShapeDtypeStruct((energies, 8, half), jnp.int32),
        ],
        (
            *in_place(tiles, offsets),
            first_step,
            later_steps,
            great_sources,
            lower_great,
            great_total,
            chip_great,
            lower_whole,
            whole,
            chip_whole,
            lessers,
        ),
        3 * unit,
        in_specs=[HBM] * 2 + [VMEM] * 10,
        scratch=[pltpu.VMEM((blocks, order, 2 * order), BF16)] * 2
        + [
            pltpu.SMEM(tiles.shape, jnp.int32),
            pltpu.SMEM(offsets.shape, jnp.int32),
            pltpu.SemaphoreType.DMA((2,)),
        ],
    )

    taken = swap(given)

    def step_on(z, state, kept, source):
        return kernel_call(
            functools.partial(advance_kernel, z),
            [block, block],
            (state, chip_whole, source, *kept),
            2 * unit,
        )

    def keep_last(state, kept):
        return kernel_call(
            functools.partial(keep_kernel, chips - 1), [block], (state, *kept), 0
        )

    less, great = joined_less, chip_great
    less_in, great_in = (), ()
    for z in range(1, chips):
        less, great = hop(less, z), hop(great, z)
        if z < chips - 1:
            less, *less_in = step_on(z, less, less_in, chip_less)
            great, *great_in = step_on(z, great, great_in, chip_great)
        else:
            less_in = keep_last(less, less_in)
            great_in = keep_last(great, great_in)
    pieces = kernel_call(
        functools.partial(finish_kernel, energies),
        [jax.ShapeDtypeStruct((2, rows, order), BF16)] * energies,
        (swap(*less_in), *great_in, given, taken, own_parts),
        6 * unit,
        scratch=[pltpu.VMEM((2 * order, 2 * order), BF16)],
    )
    pieces = [pieces[0]] + [across(pieces[k], k) for k in range(1, energies)]
    (packed,) = kernel_call(
        functools.partial(pack_kernel, energies),
        [jax.ShapeDtypeStruct((energies, rows, order), BF16)],
        pieces,
        0,
    )
    shares = kernel_call(
        functools.partial(convolve_kernel, energies),
        [piece] * energies,
        (shifts, swap(packed), *pieces),
        8 * energies * energies * rows * half,
        scratch=[pltpu.VMEM((energies, rows, order), BF16)] * 2,
    )
    shares = [shares[0]] + [across(shares[k], k) for k in range(1, energies)]
    (result,) = kernel_call(
        functools.partial(gather_kernel, energies),
        [jax.ShapeDtypeStruct((energies, rows, order), BF16)],
        shares,
        0,
        out_specs=[HBM],
        scratch=[pltpu.SemaphoreType.DMA((energies,))],
    )
    return result.reshape(1, blocks, chosen, half, order)


def solution(mesh):
    placed = (
        P("energy", "domain", None, None),
        P("domain", None, None),
        P("energy", "domain", None, None),
        P("energy", "domain", None, None),
        P("domain", None),
        P(),
    )

    return jax.shard_map(
        shards,
        mesh=mesh,
        in_specs=placed,
        out_specs=P("energy", "domain", None, None, None),
        check_vma=False,
    )
```

```python
import functools
import math

import jax
import jax.numpy as jnp
from jax import lax
from jax.experimental import pallas as pl
from jax.experimental.pallas import tpu as pltpu
from jax.sharding import PartitionSpec as P


VMEM_LIMIT = 16 << 20
F32 = jnp.float32
BF16 = jnp.bfloat16
VMEM = pl.BlockSpec(memory_space=pltpu.VMEM)
HBM = pl.BlockSpec(memory_space=pltpu.HBM)


def stacked(block):
    order = block.shape[-1] // 2
    real, imag = block[:, :order], block[:, order:]
    return jnp.concatenate([block, jnp.concatenate([-imag, real], axis=1)], axis=0)


def times(factor, second_stacked):
    return lax.dot_general(
        factor, second_stacked, (((1,), (0,)), ((), ())), preferred_element_type=F32
    )


def times_adjoint(factor, second_stacked):
    return lax.dot_general(
        factor, second_stacked, (((1,), (1,)), ((), ())), preferred_element_type=F32
    )


def product(factor, second):
    return times(factor, stacked(second)).astype(BF16)


def injected(retarded, sigma):
    return times_adjoint(product(retarded, sigma), stacked(retarded)).astype(BF16)


def advance(state, step, source):
    return (times_adjoint(product(step, state), stacked(step)) + source.astype(F32)).astype(
        BF16
    )


def kernel_call(body, outs, operands, flops, in_specs=None, scratch=(), out_specs=None):
    moved = sum(x.size * x.dtype.itemsize for x in operands)
    moved += sum(math.prod(o.shape) * o.dtype.itemsize for o in outs)
    return pl.pallas_call(
        body,
        out_shape=outs,
        in_specs=in_specs or [VMEM] * len(operands),
        out_specs=out_specs or [VMEM] * len(outs),
        scratch_shapes=list(scratch),
        compiler_params=pltpu.CompilerParams(vmem_limit_bytes=VMEM_LIMIT),
        cost_estimate=pl.CostEstimate(
            flops=int(flops), bytes_accessed=moved, transcendentals=0
        ),
    )(*operands)


class Copies:
    def __init__(self, source, target, sems):
        parts = sems.shape[0]
        rows = target.shape[0] // parts
        self.parts = [
            pltpu.make_async_copy(
                source.at[pl.ds(i * rows, rows)], target.at[pl.ds(i * rows, rows)], sems.at[i]
            )
            for i in range(parts)
        ]
        for part in self.parts:
            part.start()

    def wait(self):
        for part in self.parts:
            part.wait()


def first_kernel(
    blocks,
    retarded,
    coupling,
    lesser,
    greater,
    held_retarded,
    held_coupling,
    held_greater,
    later_steps,
    sources,
    total,
    held_lesser,
    sem,
):
    copies = {}
    for k in range(blocks):
        copies["r", k] = (retarded.at[0, k], held_retarded.at[k])
        copies["l", k] = (lesser.at[0, k], held_lesser.at[k])
        if k > 0:
            copies["c", k] = (coupling.at[k], held_coupling.at[k])
    copies["c", 0] = (coupling.at[0], held_coupling.at[0])
    for k in range(blocks):
        copies["g", k] = (greater.at[0, k], held_greater.at[k])
    for index, (key, (source, target)) in enumerate(copies.items()):
        copies[key] = Copies(source, target, sem.at[index])
    state = None
    for k in range(blocks):
        copies["r", k].wait()
        copies["l", k].wait()
        source = injected(held_retarded[k], held_lesser[k])
        sources[k] = source
        if k > 0:
            copies["c", k].wait()
            step = product(held_retarded[k], held_coupling[k])
            later_steps[k - 1] = step
        state = source if k == 0 else advance(state, step, source)
    total[...] = state
    copies["c", 0].wait()
    for k in range(blocks):
        copies["g", k].wait()


def second_kernel(
    blocks, retarded, coupling, greater, later_steps, first_step, sources, total, whole
):
    state = chain = None
    for k in range(blocks):
        source = injected(retarded[k], greater[k])
        sources[k] = source
        if k == 0:
            chain = product(retarded[0], coupling[0])
            first_step[...] = chain
            state = source
        else:
            step = later_steps[k - 1]
            chain = product(step, chain)
            state = advance(state, step, source)
    total[...] = state
    whole[...] = chain


def join_kernel(every_chip, lower, whole, upper, out):
    needed = (lax.axis_index("domain") & 1) == 1
    if not every_chip:
        needed &= (lax.axis_index("domain") >> 1) == 0

    @pl.when(needed)
    def _():
        out[...] = advance(lower[...], whole[...], upper[...])


def chain_kernel(later, earlier, out):
    out[...] = product(later[...], earlier[...])


def keep(z, state, kept, out):
    chip = lax.axis_index("domain") >> 1

    @pl.when(chip == z)
    def _():
        out[...] = state[...]

    @pl.when(chip != z)
    def _():
        out[...] = jnp.zeros_like(out) if kept is None else kept[...]


def advance_kernel(z, state, step, source, *refs):
    kept, (out, chosen) = (refs[0] if len(refs) == 3 else None), refs[-2:]
    out[...] = advance(state[...], step[...], source[...])
    keep(z, state, kept, chosen)


def keep_kernel(z, state, *refs):
    keep(z, state, refs[0] if len(refs) == 2 else None, refs[-1])


def parts_at(energies, rows, half, k):
    below = energies * (rows + half)
    return below + (k // 2) * rows, (k % 2) * 2 * half


def states_of(blocks, first_step, later_steps, sources, lower, total, chip, states):
    upper = lax.axis_index("domain") & 1

    @pl.when(upper == 0)
    def _():
        states[0] = sources[0]
        if blocks > 1:
            states[blocks - 1] = total[...]

    @pl.when(upper == 1)
    def _():
        if blocks > 1:
            states[0] = advance(lower[...], first_step[...], sources[0])
        states[blocks - 1] = chip[...]

    for k in range(1, blocks - 1):
        states[k] = advance(states[k - 1], later_steps[k - 1], sources[k])


def prepare_lesser_kernel(
    blocks,
    whole,
    joined,
    first_step,
    later_steps,
    sources,
    lower,
    total,
    states,
    chip,
):
    first_chip = (lax.axis_index("domain") >> 1) == 0

    @pl.when(first_chip)
    def _():
        chip[...] = joined[...]

    @pl.when(jnp.logical_not(first_chip))
    def _():
        chip[...] = advance(lower[...], whole[...], total[...])

    states_of(blocks, first_step, later_steps, sources, lower, total, chip, states)


def prepare_kernel(
    blocks,
    energies,
    chosen,
    tiles,
    offsets,
    first_step,
    later_steps,
    greater_sources,
    lower_great,
    great_total,
    chip_great,
    lower_whole,
    whole,
    chip_whole,
    lessers,
    given,
    own_parts,
    shifts,
    chains,
    greaters,
    held_tiles,
    held_offsets,
    sem,
):
    copies = [
        pltpu.make_async_copy(tiles, held_tiles, sem.at[0]),
        pltpu.make_async_copy(offsets, held_offsets, sem.at[1]),
    ]
    for copy in copies:
        copy.start()
    upper = lax.axis_index("domain") & 1
    group = lax.axis_index("energy")
    order = first_step.shape[0]
    half = order // 2
    rows = blocks * chosen * half // energies
    states_of(
        blocks,
        first_step,
        later_steps,
        greater_sources,
        lower_great,
        great_total,
        chip_great,
        greaters,
    )

    @pl.when(upper == 0)
    def _():
        chains[0] = first_step[...]
        chains[blocks - 1] = whole[...]

    @pl.when(upper == 1)
    def _():
        if blocks > 1:
            chains[0] = product(first_step[...], lower_whole[...])
        chains[blocks - 1] = chip_whole[...]

    for k in range(1, blocks - 1):
        chains[k] = product(later_steps[k - 1], chains[k - 1])
    for copy in copies:
        copy.wait()
    for k in range(energies):
        shifts[k] = jnp.full(shifts.shape[1:], held_offsets[group ^ k], jnp.int32)
        first = (group ^ k) * rows
        block = first // (chosen * half)
        tile = held_tiles[block, (first // half) % chosen]
        start = first % half
        row = pl.multiple_of((tile // 2) * half + start, 16)
        column = pl.multiple_of((tile % 2) * half, half)
        mine = slice(k * rows, (k + 1) * rows)
        given[mine] = chains[block, pl.ds(row, rows), :]
        others = slice(energies * rows + k * half, energies * rows + (k + 1) * half)
        given[others] = chains[block, pl.ds(column, half), :]

        def pick(states):
            return jnp.concatenate(
                [
                    states[
                        block,
                        pl.ds(row, rows),
                        pl.ds(pl.multiple_of(column + part * order, half), half),
                    ]
                    for part in range(2)
                ],
                axis=1,
            )

        base, side = parts_at(energies, rows, half, k)

        @pl.when(upper == 0)
        def _():
            own_parts[mine] = pick(lessers)
            given[base : base + rows, side : side + order] = pick(greaters)

        @pl.when(upper == 1)
        def _():
            own_parts[mine] = pick(greaters)
            given[base : base + rows, side : side + order] = pick(lessers)


def finish_kernel(
    energies, made, last, near, lesser, greater, given, taken, own_parts, *refs
):
    pieces, doubled = refs[: len(made)], refs[len(made)]
    rows, order = pieces[0].shape[1:]
    half = order // 2
    upper = lax.axis_index("domain") & 1
    at_last = (lax.axis_index("domain") >> 1) == last

    @pl.when((upper == 0) & at_last)
    def _():
        doubled[...] = stacked(lesser[...])

    @pl.when((upper == 0) & jnp.logical_not(at_last))
    def _():
        doubled[...] = stacked(near[...])

    @pl.when(upper == 1)
    def _():
        doubled[...] = stacked(greater[...])

    span = slice(made[0] * rows, (made[-1] + 1) * rows)
    for source, slot in ((given, upper), (taken, 1 - upper)):
        moved = times(source[span], doubled[...]).astype(BF16)
        for i, k in enumerate(made):
            first = energies * rows + k * half
            right = stacked(source[first : first + half])
            if source is given:
                part = own_parts[k * rows : (k + 1) * rows]
            else:
                base, side = parts_at(energies, rows, half, k)
                part = source[base : base + rows, side : side + order]
            pieces[i][slot] = (
                times_adjoint(moved[i * rows : (i + 1) * rows], right) + part.astype(F32)
            ).astype(BF16)


def pack_kernel(energies, *refs):
    pieces, out = refs[:energies], refs[energies]
    other = 1 - (lax.axis_index("domain") & 1)
    for k in range(energies):
        out[k] = pieces[k][other]


def convolve_kernel(energies, shifts, swapped, *refs):
    pieces, outs = refs[:energies], refs[energies : 2 * energies]
    upper = lax.axis_index("domain") & 1
    held_less, held_great = refs[2 * energies :]
    group = lax.axis_index("energy")
    rows, width = outs[0].shape
    half = width // 2
    reach = energies // 2

    @pl.when(upper == 0)
    def _():
        for k in range(energies):
            held_less[group ^ k] = pieces[k][0]
            held_great[group ^ k] = swapped[k]

    @pl.when(upper == 1)
    def _():
        for k in range(energies):
            held_less[group ^ k] = swapped[k]
            held_great[group ^ k] = pieces[k][1]

    chunk = 16
    for start in range(0, rows, chunk):
        at = slice(start, start + chunk)
        totals = [None] * energies
        wanted = [jnp.broadcast_to(shifts[k, :1], (chunk, half)) for k in range(energies)]
        for distance in range(-reach, reach + 1):
            real = imag = None
            for e in range(max(0, distance), min(energies, energies + distance)):
                lr = held_less[e, at, :half].astype(F32)
                li = held_less[e, at, half:].astype(F32)
                gr = held_great[e - distance, at, :half].astype(F32)
                gi = held_great[e - distance, at, half:].astype(F32)
                more_real, more_imag = lr * gr - li * gi, lr * gi + li * gr
                real = more_real if real is None else real + more_real
                imag = more_imag if imag is None else imag + more_imag
            for k in range(energies):
                if totals[k] is None:
                    totals[k] = (real, imag)
                else:
                    match = wanted[k] == distance
                    totals[k] = (
                        jnp.where(match, real, totals[k][0]),
                        jnp.where(match, imag, totals[k][1]),
                    )
        for k in range(energies):
            outs[k][at, :half] = (totals[k][0] / energies).astype(BF16)
            outs[k][at, half:] = (totals[k][1] / energies).astype(BF16)


def gather_kernel(energies, *refs):
    shares, (out, sem) = refs[:energies], refs[energies:]
    group = lax.axis_index("energy")
    copies = [
        pltpu.make_async_copy(shares[k], out.at[group ^ k], sem.at[k])
        for k in range(energies)
    ]
    for copy in copies:
        copy.start()
    for copy in copies:
        copy.wait()


def shards(retarded, coupling, sigma_lesser, sigma_greater, tiles, offsets):
    blocks, order = retarded.shape[1], retarded.shape[2]
    half = order // 2
    chosen = tiles.shape[1]
    domains, energies = lax.axis_size("domain"), lax.axis_size("energy")
    chips = domains // 2
    rows = blocks * chosen * half // energies
    unit = 8 * order**3
    block = jax.ShapeDtypeStruct((order, 2 * order), BF16)
    piece = jax.ShapeDtypeStruct((rows, order), BF16)

    def series(count):
        return jax.ShapeDtypeStruct((count, order, 2 * order), BF16)

    def in_place(*arrays):
        return tuple(pltpu.with_memory_space_constraint(x, pltpu.HBM) for x in arrays)

    def swap(x):
        return lax.ppermute(x, "domain", [(d, d ^ 1) for d in range(domains)])

    def hop(x, z, lower=False):
        source, target = 2 * z - 1, 2 * z + (not lower)
        aside = target ^ 1
        if z < chips - 1 or lower or energies % 4:
            ring = [source, target, aside, source - 1]
        else:
            ring = [source, target, source - 1]
        onward = dict(zip(ring, ring[1:] + ring[:1]))
        route = []
        for e in range(energies):
            for d in range(domains):
                if d in onward:
                    place = (e, onward[d])
                elif d == aside:
                    place = (e ^ 2, d)
                else:
                    place = (e, d ^ 1)
                route.append((e * domains + d, place[0] * domains + place[1]))
        return lax.ppermute(x, ("energy", "domain"), route)

    def across(x, k):
        return lax.ppermute(x, "energy", [(e, e ^ k) for e in range(energies)])

    held_retarded, held_coupling, held_greater, later_steps, less_sources, less_total = (
        kernel_call(
            functools.partial(first_kernel, blocks),
            [series(blocks)] * 3 + [series(blocks - 1), series(blocks), block],
            in_place(retarded, coupling, sigma_lesser, sigma_greater),
            (5 * blocks - 3) * unit,
            in_specs=[HBM] * 4,
            scratch=[
                pltpu.VMEM((blocks, order, 2 * order), BF16),
                pltpu.SemaphoreType.DMA((4 * blocks, 2)),
            ],
        )
    )
    lower_less = swap(less_total)
    first_step, great_sources, great_total, whole = kernel_call(
        functools.partial(second_kernel, blocks),
        [block, series(blocks), block, block],
        (held_retarded, held_coupling, held_greater, later_steps),
        (5 * blocks - 2) * unit,
    )
    lower_great = swap(great_total)
    lower_whole = swap(whole)
    (joined_less,) = kernel_call(
        functools.partial(join_kernel, False),
        [block],
        (lower_less, whole, less_total),
        2 * unit,
    )
    (chip_great,) = kernel_call(
        functools.partial(join_kernel, True),
        [block],
        (lower_great, whole, great_total),
        2 * unit,
    )
    (chip_whole,) = kernel_call(chain_kernel, [block], (whole, lower_whole), unit)
    lessers, chip_less = kernel_call(
        functools.partial(prepare_lesser_kernel, blocks),
        [series(blocks), block],
        (whole, joined_less, first_step, later_steps, less_sources, lower_less, less_total),
        4 * unit,
    )
    given, own_parts, shifts = kernel_call(
        functools.partial(prepare_kernel, blocks, energies, chosen),
        [
            jax.ShapeDtypeStruct(
                (energies * (rows + half) + pl.cdiv(energies, 2) * rows, 2 * order), BF16
            ),
            jax.ShapeDtypeStruct((energies * rows, order), BF16),
            jax.ShapeDtypeStruct((energies, 8, half), jnp.int32),
        ],
        (
            *in_place(tiles, offsets),
            first_step,
            later_steps,
            great_sources,
            lower_great,
            great_total,
            chip_great,
            lower_whole,
            whole,
            chip_whole,
            lessers,
        ),
        3 * unit,
        in_specs=[HBM] * 2 + [VMEM] * 10,
        scratch=[pltpu.VMEM((blocks, order, 2 * order), BF16)] * 2
        + [
            pltpu.SMEM(tiles.shape, jnp.int32),
            pltpu.SMEM(offsets.shape, jnp.int32),
            pltpu.SemaphoreType.DMA((2,)),
        ],
    )

    taken = swap(given)

    def step_on(z, state, kept, source):
        return kernel_call(
            functools.partial(advance_kernel, z),
            [block, block],
            (state, chip_whole, source, *kept),
            2 * unit,
        )

    def keep_last(state, kept):
        return kernel_call(
            functools.partial(keep_kernel, chips - 1), [block], (state, *kept), 0
        )

    less, great = joined_less, chip_great
    less_in, great_in = (), ()
    for z in range(1, chips):
        less = hop(less, z, lower=z == chips - 1)
        great = hop(great, z)
        if z < chips - 1:
            less, *less_in = step_on(z, less, less_in, chip_less)
            great, *great_in = step_on(z, great, great_in, chip_great)
        else:
            great_in = keep_last(great, great_in)
    near = swap(*less_in) if less_in else jnp.zeros_like(less)

    def finish(made):
        return kernel_call(
            functools.partial(finish_kernel, energies, made, chips - 1),
            [jax.ShapeDtypeStruct((2, rows, order), BF16)] * len(made),
            (near, less, *great_in, given, taken, own_parts),
            6 * len(made) / energies * unit,
            scratch=[pltpu.VMEM((2 * order, 2 * order), BF16)],
        )

    pieces = finish(range(1, energies))
    pieces = [across(piece, k + 1) for k, piece in enumerate(pieces)]
    pieces = [*finish(range(1)), *pieces]
    (packed,) = kernel_call(
        functools.partial(pack_kernel, energies),
        [jax.ShapeDtypeStruct((energies, rows, order), BF16)],
        pieces,
        0,
    )
    shares = kernel_call(
        functools.partial(convolve_kernel, energies),
        [piece] * energies,
        (shifts, swap(packed), *pieces),
        8 * energies * energies * rows * half,
        scratch=[pltpu.VMEM((energies, rows, order), BF16)] * 2,
    )
    shares = [shares[0]] + [across(shares[k], k) for k in range(1, energies)]
    (result,) = kernel_call(
        functools.partial(gather_kernel, energies),
        [jax.ShapeDtypeStruct((energies, rows, order), BF16)],
        shares,
        0,
        out_specs=[HBM],
        scratch=[pltpu.SemaphoreType.DMA((energies,))],
    )
    return result.reshape(1, blocks, chosen, half, order)


def solution(mesh):
    placed = (
        P("energy", "domain", None, None),
        P("domain", None, None),
        P("energy", "domain", None, None),
        P("energy", "domain", None, None),
        P("domain", None),
        P(),
    )

    return jax.shard_map(
        shards,
        mesh=mesh,
        in_specs=placed,
        out_specs=P("energy", "domain", None, None, None),
        check_vma=False,
    )
```

```python
import functools
import math

import jax
import jax.numpy as jnp
from jax import lax
from jax.experimental import pallas as pl
from jax.experimental.pallas import tpu as pltpu
from jax.sharding import PartitionSpec as P


VMEM_LIMIT = 16 << 20
F32 = jnp.float32
BF16 = jnp.bfloat16
VMEM = pl.BlockSpec(memory_space=pltpu.VMEM)
HBM = pl.BlockSpec(memory_space=pltpu.HBM)


def stacked(block):
    order = block.shape[-1] // 2
    real, imag = block[:, :order], block[:, order:]
    return jnp.concatenate([block, jnp.concatenate([-imag, real], axis=1)], axis=0)


def times(factor, second_stacked):
    return lax.dot_general(
        factor, second_stacked, (((1,), (0,)), ((), ())), preferred_element_type=F32
    )


def times_adjoint(factor, second_stacked):
    return lax.dot_general(
        factor, second_stacked, (((1,), (1,)), ((), ())), preferred_element_type=F32
    )


def product(factor, second):
    return times(factor, stacked(second)).astype(BF16)


def injected(retarded, sigma):
    return times_adjoint(product(retarded, sigma), stacked(retarded)).astype(BF16)


def advance(state, step, source):
    return (times_adjoint(product(step, state), stacked(step)) + source.astype(F32)).astype(
        BF16
    )


def kernel_call(
    body, outs, operands, flops, in_specs=None, scratch=(), out_specs=None, aliases=None
):
    moved = sum(x.size * x.dtype.itemsize for x in operands)
    moved += sum(math.prod(o.shape) * o.dtype.itemsize for o in outs)
    return pl.pallas_call(
        body,
        out_shape=outs,
        in_specs=in_specs or [VMEM] * len(operands),
        out_specs=out_specs or [VMEM] * len(outs),
        scratch_shapes=list(scratch),
        input_output_aliases=aliases or {},
        compiler_params=pltpu.CompilerParams(vmem_limit_bytes=VMEM_LIMIT),
        cost_estimate=pl.CostEstimate(
            flops=int(flops), bytes_accessed=moved, transcendentals=0
        ),
    )(*operands)


class Copies:
    def __init__(self, source, target, sems):
        parts = sems.shape[0]
        rows = target.shape[0] // parts
        self.parts = [
            pltpu.make_async_copy(
                source.at[pl.ds(i * rows, rows)], target.at[pl.ds(i * rows, rows)], sems.at[i]
            )
            for i in range(parts)
        ]
        for part in self.parts:
            part.start()

    def wait(self):
        for part in self.parts:
            part.wait()


def first_kernel(
    blocks,
    retarded,
    coupling,
    lesser,
    greater,
    held_retarded,
    held_coupling,
    held_greater,
    later_steps,
    sources,
    total,
    held_lesser,
    sem,
):
    copies = {}
    for k in range(blocks):
        copies["r", k] = (retarded.at[0, k], held_retarded.at[k])
        copies["l", k] = (lesser.at[0, k], held_lesser.at[k])
        if k > 0:
            copies["c", k] = (coupling.at[k], held_coupling.at[k])
    copies["c", 0] = (coupling.at[0], held_coupling.at[0])
    for k in range(blocks):
        copies["g", k] = (greater.at[0, k], held_greater.at[k])
    for index, (key, (source, target)) in enumerate(copies.items()):
        copies[key] = Copies(source, target, sem.at[index])
    state = None
    for k in range(blocks):
        copies["r", k].wait()
        copies["l", k].wait()
        source = injected(held_retarded[k], held_lesser[k])
        sources[k] = source
        if k > 0:
            copies["c", k].wait()
            step = product(held_retarded[k], held_coupling[k])
            later_steps[k - 1] = step
        state = source if k == 0 else advance(state, step, source)
    total[...] = state
    copies["c", 0].wait()
    for k in range(blocks):
        copies["g", k].wait()


def second_kernel(
    blocks, retarded, coupling, greater, later_steps, first_step, sources, total, whole
):
    state = chain = None
    for k in range(blocks):
        source = injected(retarded[k], greater[k])
        sources[k] = source
        if k == 0:
            chain = product(retarded[0], coupling[0])
            first_step[...] = chain
            state = source
        else:
            step = later_steps[k - 1]
            chain = product(step, chain)
            state = advance(state, step, source)
    total[...] = state
    whole[...] = chain


def join_kernel(every_chip, lower, whole, upper, out):
    needed = (lax.axis_index("domain") & 1) == 1
    if not every_chip:
        needed &= (lax.axis_index("domain") >> 1) == 0

    @pl.when(needed)
    def _():
        out[...] = advance(lower[...], whole[...], upper[...])


def chain_kernel(later, earlier, out):
    out[...] = product(later[...], earlier[...])


def keep(z, state, kept, out):
    chip = lax.axis_index("domain") >> 1

    @pl.when(chip == z)
    def _():
        out[...] = state[...]

    @pl.when(chip != z)
    def _():
        out[...] = jnp.zeros_like(out) if kept is None else kept[...]


def advance_kernel(z, state, step, source, *refs):
    kept, (out, chosen) = (refs[0] if len(refs) == 3 else None), refs[-2:]
    out[...] = advance(state[...], step[...], source[...])
    keep(z, state, kept, chosen)


def parts_at(energies, rows, half, k):
    below = energies * (rows + half)
    return below + (k // 2) * rows, (k % 2) * 2 * half


def states_of(blocks, first_step, later_steps, sources, lower, total, chip, states):
    upper = lax.axis_index("domain") & 1

    @pl.when(upper == 0)
    def _():
        states[0] = sources[0]
        if blocks > 1:
            states[blocks - 1] = total[...]

    @pl.when(upper == 1)
    def _():
        if blocks > 1:
            states[0] = advance(lower[...], first_step[...], sources[0])
        states[blocks - 1] = chip[...]

    for k in range(1, blocks - 1):
        states[k] = advance(states[k - 1], later_steps[k - 1], sources[k])


def prepare_lesser_kernel(
    blocks,
    whole,
    joined,
    first_step,
    later_steps,
    sources,
    lower,
    total,
    states,
    chip,
):
    first_chip = (lax.axis_index("domain") >> 1) == 0

    @pl.when(first_chip)
    def _():
        chip[...] = joined[...]

    @pl.when(jnp.logical_not(first_chip))
    def _():
        chip[...] = advance(lower[...], whole[...], total[...])

    states_of(blocks, first_step, later_steps, sources, lower, total, chip, states)


def prepare_kernel(
    blocks,
    energies,
    chosen,
    tiles,
    offsets,
    first_step,
    later_steps,
    greater_sources,
    lower_great,
    great_total,
    chip_great,
    lower_whole,
    whole,
    chip_whole,
    lessers,
    given,
    own_parts,
    shifts,
    chains,
    greaters,
    held_tiles,
    held_offsets,
    sem,
):
    copies = [
        pltpu.make_async_copy(tiles, held_tiles, sem.at[0]),
        pltpu.make_async_copy(offsets, held_offsets, sem.at[1]),
    ]
    for copy in copies:
        copy.start()
    upper = lax.axis_index("domain") & 1
    group = lax.axis_index("energy")
    order = first_step.shape[0]
    half = order // 2
    rows = blocks * chosen * half // energies
    states_of(
        blocks,
        first_step,
        later_steps,
        greater_sources,
        lower_great,
        great_total,
        chip_great,
        greaters,
    )

    @pl.when(upper == 0)
    def _():
        chains[0] = first_step[...]
        chains[blocks - 1] = whole[...]

    @pl.when(upper == 1)
    def _():
        if blocks > 1:
            chains[0] = product(first_step[...], lower_whole[...])
        chains[blocks - 1] = chip_whole[...]

    for k in range(1, blocks - 1):
        chains[k] = product(later_steps[k - 1], chains[k - 1])
    for copy in copies:
        copy.wait()
    for k in range(energies):
        shifts[k] = jnp.full(shifts.shape[1:], held_offsets[group ^ k], jnp.int32)
        first = (group ^ k) * rows
        block = first // (chosen * half)
        tile = held_tiles[block, (first // half) % chosen]
        start = first % half
        row = pl.multiple_of((tile // 2) * half + start, 16)
        column = pl.multiple_of((tile % 2) * half, half)
        mine = slice(k * rows, (k + 1) * rows)
        given[mine] = chains[block, pl.ds(row, rows), :]
        others = slice(energies * rows + k * half, energies * rows + (k + 1) * half)
        given[others] = chains[block, pl.ds(column, half), :]

        def pick(states):
            return jnp.concatenate(
                [
                    states[
                        block,
                        pl.ds(row, rows),
                        pl.ds(pl.multiple_of(column + part * order, half), half),
                    ]
                    for part in range(2)
                ],
                axis=1,
            )

        base, side = parts_at(energies, rows, half, k)

        @pl.when(upper == 0)
        def _():
            own_parts[mine] = pick(lessers)
            given[base : base + rows, side : side + order] = pick(greaters)

        @pl.when(upper == 1)
        def _():
            own_parts[mine] = pick(greaters)
            given[base : base + rows, side : side + order] = pick(lessers)


def tiles_kernel(energies, made, greater, lesser, given, taken, own_parts, pieces, doubled):
    rows, order = pieces[0].shape[1:]
    half = order // 2
    upper = lax.axis_index("domain") & 1

    @pl.when(upper == 0)
    def _():
        doubled[...] = stacked(lesser[...])

    @pl.when(upper == 1)
    def _():
        doubled[...] = stacked(greater[...])

    span = slice(made[0] * rows, (made[-1] + 1) * rows)
    for source, slot in ((given, upper), (taken, 1 - upper)):
        moved = times(source[span], doubled[...]).astype(BF16)
        for i, k in enumerate(made):
            first = energies * rows + k * half
            right = stacked(source[first : first + half])
            if source is given:
                part = own_parts[k * rows : (k + 1) * rows]
            else:
                base, side = parts_at(energies, rows, half, k)
                part = source[base : base + rows, side : side + order]
            pieces[i][slot] = (
                times_adjoint(moved[i * rows : (i + 1) * rows], right) + part.astype(F32)
            ).astype(BF16)


def finish_kernel(energies, made, last, on_last, lesser, greater, *refs):
    operands, refs = refs[:3], refs[3:]
    pieces, doubled = refs[-1 - len(made) : -1], refs[-1]
    at_last = (lax.axis_index("domain") >> 1) == last

    @pl.when(at_last if on_last else jnp.logical_not(at_last))
    def _():
        tiles_kernel(energies, made, greater, lesser, *operands, pieces, doubled)


def finish_own_kernel(energies, last, near, kept, lesser, greater, *refs):
    operands, (piece, doubled, arrived_less, arrived_great) = refs[:3], refs[3:]
    at_last = (lax.axis_index("domain") >> 1) == last

    @pl.when(at_last)
    def _():
        arrived_less[...] = lesser[...]
        arrived_great[...] = greater[...]

    @pl.when(jnp.logical_not(at_last))
    def _():
        arrived_less[...] = near[...]
        arrived_great[...] = kept[...]

    tiles_kernel(
        energies, range(1), arrived_great, arrived_less, *operands, [piece], doubled
    )


def pack_kernel(energies, *refs):
    pieces, out = refs[:energies], refs[energies]
    other = 1 - (lax.axis_index("domain") & 1)
    for k in range(energies):
        out[k] = pieces[k][other]


def convolve_kernel(energies, shifts, swapped, *refs):
    pieces, outs = refs[:energies], refs[energies : 2 * energies]
    upper = lax.axis_index("domain") & 1
    held_less, held_great = refs[2 * energies :]
    group = lax.axis_index("energy")
    rows, width = outs[0].shape
    half = width // 2
    reach = energies // 2

    @pl.when(upper == 0)
    def _():
        for k in range(energies):
            held_less[group ^ k] = pieces[k][0]
            held_great[group ^ k] = swapped[k]

    @pl.when(upper == 1)
    def _():
        for k in range(energies):
            held_less[group ^ k] = swapped[k]
            held_great[group ^ k] = pieces[k][1]

    chunk = 16
    for start in range(0, rows, chunk):
        at = slice(start, start + chunk)
        totals = [None] * energies
        wanted = [jnp.broadcast_to(shifts[k, :1], (chunk, half)) for k in range(energies)]
        for distance in range(-reach, reach + 1):
            real = imag = None
            for e in range(max(0, distance), min(energies, energies + distance)):
                lr = held_less[e, at, :half].astype(F32)
                li = held_less[e, at, half:].astype(F32)
                gr = held_great[e - distance, at, :half].astype(F32)
                gi = held_great[e - distance, at, half:].astype(F32)
                more_real, more_imag = lr * gr - li * gi, lr * gi + li * gr
                real = more_real if real is None else real + more_real
                imag = more_imag if imag is None else imag + more_imag
            for k in range(energies):
                if totals[k] is None:
                    totals[k] = (real, imag)
                else:
                    match = wanted[k] == distance
                    totals[k] = (
                        jnp.where(match, real, totals[k][0]),
                        jnp.where(match, imag, totals[k][1]),
                    )
        for k in range(energies):
            outs[k][at, :half] = (totals[k][0] / energies).astype(BF16)
            outs[k][at, half:] = (totals[k][1] / energies).astype(BF16)


def gather_kernel(energies, *refs):
    shares, (out, sem) = refs[:energies], refs[energies:]
    group = lax.axis_index("energy")
    copies = [
        pltpu.make_async_copy(shares[k], out.at[group ^ k], sem.at[k])
        for k in range(energies)
    ]
    for copy in copies:
        copy.start()
    for copy in copies:
        copy.wait()


def shards(retarded, coupling, sigma_lesser, sigma_greater, tiles, offsets):
    blocks, order = retarded.shape[1], retarded.shape[2]
    half = order // 2
    chosen = tiles.shape[1]
    domains, energies = lax.axis_size("domain"), lax.axis_size("energy")
    chips = domains // 2
    rows = blocks * chosen * half // energies
    unit = 8 * order**3
    block = jax.ShapeDtypeStruct((order, 2 * order), BF16)
    piece = jax.ShapeDtypeStruct((rows, order), BF16)

    def series(count):
        return jax.ShapeDtypeStruct((count, order, 2 * order), BF16)

    def in_place(*arrays):
        return tuple(pltpu.with_memory_space_constraint(x, pltpu.HBM) for x in arrays)

    def swap(x):
        return lax.ppermute(x, "domain", [(d, d ^ 1) for d in range(domains)])

    def hop(x, z, lower=False):
        source, target = 2 * z - 1, 2 * z + (not lower)
        aside = target ^ 1
        if z < chips - 1 or lower or energies % 4:
            ring = [source, target, aside, source - 1]
        else:
            ring = [source, target, source - 1]
        onward = dict(zip(ring, ring[1:] + ring[:1]))
        route = []
        for e in range(energies):
            for d in range(domains):
                if d in onward:
                    place = (e, onward[d])
                elif d == aside:
                    place = (e ^ 2, d)
                else:
                    place = (e, d ^ 1)
                route.append((e * domains + d, place[0] * domains + place[1]))
        return lax.ppermute(x, ("energy", "domain"), route)

    def across(x, k):
        return lax.ppermute(x, "energy", [(e, e ^ k) for e in range(energies)])

    held_retarded, held_coupling, held_greater, later_steps, less_sources, less_total = (
        kernel_call(
            functools.partial(first_kernel, blocks),
            [series(blocks)] * 3 + [series(blocks - 1), series(blocks), block],
            in_place(retarded, coupling, sigma_lesser, sigma_greater),
            (5 * blocks - 3) * unit,
            in_specs=[HBM] * 4,
            scratch=[
                pltpu.VMEM((blocks, order, 2 * order), BF16),
                pltpu.SemaphoreType.DMA((4 * blocks, 2)),
            ],
        )
    )
    lower_less = swap(less_total)
    first_step, great_sources, great_total, whole = kernel_call(
        functools.partial(second_kernel, blocks),
        [block, series(blocks), block, block],
        (held_retarded, held_coupling, held_greater, later_steps),
        (5 * blocks - 2) * unit,
    )
    lower_great = swap(great_total)
    lower_whole = swap(whole)
    (joined_less,) = kernel_call(
        functools.partial(join_kernel, False),
        [block],
        (lower_less, whole, less_total),
        2 * unit,
    )
    (chip_great,) = kernel_call(
        functools.partial(join_kernel, True),
        [block],
        (lower_great, whole, great_total),
        2 * unit,
    )
    (chip_whole,) = kernel_call(chain_kernel, [block], (whole, lower_whole), unit)
    lessers, chip_less = kernel_call(
        functools.partial(prepare_lesser_kernel, blocks),
        [series(blocks), block],
        (whole, joined_less, first_step, later_steps, less_sources, lower_less, less_total),
        4 * unit,
    )
    given, own_parts, shifts = kernel_call(
        functools.partial(prepare_kernel, blocks, energies, chosen),
        [
            jax.ShapeDtypeStruct(
                (energies * (rows + half) + pl.cdiv(energies, 2) * rows, 2 * order), BF16
            ),
            jax.ShapeDtypeStruct((energies * rows, order), BF16),
            jax.ShapeDtypeStruct((energies, 8, half), jnp.int32),
        ],
        (
            *in_place(tiles, offsets),
            first_step,
            later_steps,
            great_sources,
            lower_great,
            great_total,
            chip_great,
            lower_whole,
            whole,
            chip_whole,
            lessers,
        ),
        3 * unit,
        in_specs=[HBM] * 2 + [VMEM] * 10,
        scratch=[pltpu.VMEM((blocks, order, 2 * order), BF16)] * 2
        + [
            pltpu.SMEM(tiles.shape, jnp.int32),
            pltpu.SMEM(offsets.shape, jnp.int32),
            pltpu.SemaphoreType.DMA((2,)),
        ],
    )

    taken = swap(given)

    def step_on(z, state, kept, source):
        return kernel_call(
            functools.partial(advance_kernel, z),
            [block, block],
            (state, chip_whole, source, *kept),
            2 * unit,
        )

    less, great = joined_less, chip_great
    less_in, great_in = (), ()
    for z in range(1, chips):
        less = hop(less, z, lower=z == chips - 1)
        great = hop(great, z)
        if z < chips - 1:
            less, *less_in = step_on(z, less, less_in, chip_less)
            great, *great_in = step_on(z, great, great_in, chip_great)
    if not less_in:
        less_in, great_in = [jnp.zeros_like(less)], [jnp.zeros_like(great)]
    near, kept = swap(*less_in), great_in[0]
    shared = (given, taken, own_parts)
    double = pltpu.VMEM((2 * order, 2 * order), BF16)
    sent = range(1, energies)
    pair = jax.ShapeDtypeStruct((2, rows, order), BF16)
    pieces = ()
    for on_last, arrived in ((False, (near, kept)), (True, (less, great))):
        operands = (*arrived, *shared, *pieces)
        pieces = kernel_call(
            functools.partial(finish_kernel, energies, sent, chips - 1, on_last),
            [pair] * len(sent),
            operands,
            5 * unit,
            scratch=[double],
            aliases={len(operands) - len(pieces) + i: i for i in range(len(pieces))},
        )
    pieces = [across(piece, k) for k, piece in zip(sent, pieces)]
    (own,) = kernel_call(
        functools.partial(finish_own_kernel, energies, chips - 1),
        [pair],
        (near, kept, less, great, *shared),
        2 * unit,
        scratch=[double] + [pltpu.VMEM((order, 2 * order), BF16)] * 2,
    )
    pieces = [own, *pieces]
    (packed,) = kernel_call(
        functools.partial(pack_kernel, energies),
        [jax.ShapeDtypeStruct((energies, rows, order), BF16)],
        pieces,
        0,
    )
    shares = kernel_call(
        functools.partial(convolve_kernel, energies),
        [piece] * energies,
        (shifts, swap(packed), *pieces),
        8 * energies * energies * rows * half,
        scratch=[pltpu.VMEM((energies, rows, order), BF16)] * 2,
    )
    shares = [shares[0]] + [across(shares[k], k) for k in range(1, energies)]
    (result,) = kernel_call(
        functools.partial(gather_kernel, energies),
        [jax.ShapeDtypeStruct((energies, rows, order), BF16)],
        shares,
        0,
        out_specs=[HBM],
        scratch=[pltpu.SemaphoreType.DMA((energies,))],
    )
    return result.reshape(1, blocks, chosen, half, order)


def solution(mesh):
    placed = (
        P("energy", "domain", None, None),
        P("domain", None, None),
        P("energy", "domain", None, None),
        P("energy", "domain", None, None),
        P("domain", None),
        P(),
    )

    return jax.shard_map(
        shards,
        mesh=mesh,
        in_specs=placed,
        out_specs=P("energy", "domain", None, None, None),
        check_vma=False,
    )
```

```python
import functools
import math

import jax
import jax.numpy as jnp
from jax import lax
from jax.experimental import pallas as pl
from jax.experimental.pallas import tpu as pltpu
from jax.sharding import PartitionSpec as P


VMEM_LIMIT = 16 << 20
F32 = jnp.float32
BF16 = jnp.bfloat16
VMEM = pl.BlockSpec(memory_space=pltpu.VMEM)
HBM = pl.BlockSpec(memory_space=pltpu.HBM)


def stacked(block):
    order = block.shape[-1] // 2
    real, imag = block[:, :order], block[:, order:]
    return jnp.concatenate([block, jnp.concatenate([-imag, real], axis=1)], axis=0)


def times(factor, second_stacked):
    return lax.dot_general(
        factor, second_stacked, (((1,), (0,)), ((), ())), preferred_element_type=F32
    )


def times_adjoint(factor, second_stacked):
    return lax.dot_general(
        factor, second_stacked, (((1,), (1,)), ((), ())), preferred_element_type=F32
    )


def product(factor, second):
    return times(factor, stacked(second)).astype(BF16)


def injected(retarded, sigma):
    return times_adjoint(product(retarded, sigma), stacked(retarded)).astype(BF16)


def advance(state, step, source):
    return (times_adjoint(product(step, state), stacked(step)) + source.astype(F32)).astype(
        BF16
    )


def kernel_call(
    body, outs, operands, flops, in_specs=None, scratch=(), out_specs=None, aliases=None
):
    moved = sum(x.size * x.dtype.itemsize for x in operands)
    moved += sum(math.prod(o.shape) * o.dtype.itemsize for o in outs)
    return pl.pallas_call(
        body,
        out_shape=outs,
        in_specs=in_specs or [VMEM] * len(operands),
        out_specs=out_specs or [VMEM] * len(outs),
        scratch_shapes=list(scratch),
        input_output_aliases=aliases or {},
        compiler_params=pltpu.CompilerParams(vmem_limit_bytes=VMEM_LIMIT),
        cost_estimate=pl.CostEstimate(
            flops=int(flops), bytes_accessed=moved, transcendentals=0
        ),
    )(*operands)


class Copies:
    def __init__(self, source, target, sems):
        parts = sems.shape[0]
        rows = target.shape[0] // parts
        self.parts = [
            pltpu.make_async_copy(
                source.at[pl.ds(i * rows, rows)], target.at[pl.ds(i * rows, rows)], sems.at[i]
            )
            for i in range(parts)
        ]
        for part in self.parts:
            part.start()

    def wait(self):
        for part in self.parts:
            part.wait()


def on_first_chip():
    return (lax.axis_index("domain") >> 1) == 0


def lesser_chain(blocks, retarded, coupling, sigma, later_steps, sources, total, ready):
    state = None
    for k in range(blocks):
        ready("r", k)
        ready("l", k)
        source = injected(retarded[k], sigma[k])
        sources[k] = source
        if k > 0:
            ready("c", k)
            step = product(retarded[k], coupling[k])
            later_steps[k - 1] = step
        state = source if k == 0 else advance(state, step, source)
    total[...] = state


def greater_chain(
    blocks, retarded, coupling, sigma, later_steps, first_step, sources, total, whole
):
    state = chain = None
    for k in range(blocks):
        source = injected(retarded[k], sigma[k])
        sources[k] = source
        if k == 0:
            chain = product(retarded[0], coupling[0])
            first_step[...] = chain
            state = source
        else:
            step = later_steps[k - 1]
            chain = product(step, chain)
            state = advance(state, step, source)
    total[...] = state
    whole[...] = chain


def first_kernel(
    blocks,
    retarded,
    coupling,
    lesser,
    greater,
    held_retarded,
    held_coupling,
    held_lesser,
    held_greater,
    later_steps,
    sources,
    total,
    sem,
):
    copies = {}
    for k in range(blocks):
        copies["r", k] = (retarded.at[0, k], held_retarded.at[k])
        copies["l", k] = (lesser.at[0, k], held_lesser.at[k])
        if k > 0:
            copies["c", k] = (coupling.at[k], held_coupling.at[k])
    copies["c", 0] = (coupling.at[0], held_coupling.at[0])
    for k in range(blocks):
        copies["g", k] = (greater.at[0, k], held_greater.at[k])
    for index, (key, (source, target)) in enumerate(copies.items()):
        copies[key] = Copies(source, target, sem.at[index])
    early = [key for key in copies if key[0] in "rl" or (key[0] == "c" and key[1] > 0)]
    first_chip = on_first_chip()

    @pl.when(first_chip)
    def _():
        lesser_chain(
            blocks,
            held_retarded,
            held_coupling,
            held_lesser,
            later_steps,
            sources,
            total,
            lambda *key: copies[key].wait(),
        )

    @pl.when(jnp.logical_not(first_chip))
    def _():
        for key in early:
            copies[key].wait()

    for key in copies:
        if key not in early:
            copies[key].wait()


def second_kernel(
    blocks,
    retarded,
    coupling,
    lesser,
    greater,
    given_steps,
    given_sources,
    given_total,
    later_steps,
    less_sources,
    less_total,
    first_step,
    great_sources,
    great_total,
    whole,
):
    first_chip = on_first_chip()

    @pl.when(first_chip)
    def _():
        greater_chain(
            blocks,
            retarded,
            coupling,
            greater,
            given_steps,
            first_step,
            great_sources,
            great_total,
            whole,
        )
        less_total[...] = given_total[...]

    @pl.when(jnp.logical_not(first_chip))
    def _():
        lesser_chain(
            blocks,
            retarded,
            coupling,
            lesser,
            later_steps,
            less_sources,
            less_total,
            lambda *key: None,
        )


def third_kernel(
    blocks,
    retarded,
    coupling,
    greater,
    later_steps,
    given_step,
    given_sources,
    given_total,
    given_whole,
    first_step,
    sources,
    total,
    whole,
):
    first_chip = on_first_chip()

    @pl.when(first_chip)
    def _():
        total[...] = given_total[...]
        whole[...] = given_whole[...]

    @pl.when(jnp.logical_not(first_chip))
    def _():
        greater_chain(
            blocks,
            retarded,
            coupling,
            greater,
            later_steps,
            first_step,
            sources,
            total,
            whole,
        )


def join_first_kernel(lower, whole, upper, out):
    @pl.when(lax.axis_index("domain") == 1)
    def _():
        out[...] = advance(lower[...], whole[...], upper[...])


def join_kernel(joined, lower, lower_whole, whole, upper, chip, chip_whole):
    on_upper = (lax.axis_index("domain") & 1) == 1
    first_chip = on_first_chip()

    @pl.when(on_upper)
    def _():
        chip_whole[...] = product(whole[...], lower_whole[...])

    @pl.when(on_upper & first_chip)
    def _():
        chip[...] = joined[...]

    @pl.when(on_upper & jnp.logical_not(first_chip))
    def _():
        chip[...] = advance(lower[...], whole[...], upper[...])


def keep(z, state, kept, out):
    chip = lax.axis_index("domain") >> 1

    @pl.when(chip == z)
    def _():
        out[...] = state[...]

    @pl.when(chip != z)
    def _():
        out[...] = jnp.zeros_like(out) if kept is None else kept[...]


def advance_kernel(z, state, step, source, *refs):
    kept, (out, chosen) = (refs[0] if len(refs) == 3 else None), refs[-2:]

    @pl.when((lax.axis_index("domain") >> 1) == z)
    def _():
        out[...] = advance(state[...], step[...], source[...])

    keep(z, state, kept, chosen)


def parts_at(energies, rows, half, k):
    below = energies * (rows + half)
    return below + (k // 2) * rows, (k % 2) * 2 * half


def states_of(blocks, first_step, later_steps, sources, lower, total, chip, states):
    upper = lax.axis_index("domain") & 1

    @pl.when(upper == 0)
    def _():
        states[0] = sources[0]
        if blocks > 1:
            states[blocks - 1] = total[...]

    @pl.when(upper == 1)
    def _():
        if blocks > 1:
            states[0] = advance(lower[...], first_step[...], sources[0])
        states[blocks - 1] = chip[...]

    for k in range(1, blocks - 1):
        states[k] = advance(states[k - 1], later_steps[k - 1], sources[k])


def prepare_lesser_kernel(
    blocks,
    whole,
    joined,
    first_step,
    later_steps,
    sources,
    lower,
    total,
    states,
    chip,
):
    first_chip = on_first_chip()

    @pl.when(first_chip)
    def _():
        chip[...] = joined[...]

    @pl.when(jnp.logical_not(first_chip))
    def _():
        chip[...] = advance(lower[...], whole[...], total[...])

    states_of(blocks, first_step, later_steps, sources, lower, total, chip, states)


def prepare_kernel(
    blocks,
    energies,
    chosen,
    tiles,
    offsets,
    first_step,
    later_steps,
    greater_sources,
    lower_great,
    great_total,
    chip_great,
    lower_whole,
    whole,
    chip_whole,
    lessers,
    given,
    own_parts,
    shifts,
    chains,
    greaters,
    held_tiles,
    held_offsets,
    sem,
):
    copies = [
        pltpu.make_async_copy(tiles, held_tiles, sem.at[0]),
        pltpu.make_async_copy(offsets, held_offsets, sem.at[1]),
    ]
    for copy in copies:
        copy.start()
    upper = lax.axis_index("domain") & 1
    group = lax.axis_index("energy")
    order = first_step.shape[0]
    half = order // 2
    rows = blocks * chosen * half // energies
    states_of(
        blocks,
        first_step,
        later_steps,
        greater_sources,
        lower_great,
        great_total,
        chip_great,
        greaters,
    )

    @pl.when(upper == 0)
    def _():
        chains[0] = first_step[...]
        chains[blocks - 1] = whole[...]

    @pl.when(upper == 1)
    def _():
        if blocks > 1:
            chains[0] = product(first_step[...], lower_whole[...])
        chains[blocks - 1] = chip_whole[...]

    for k in range(1, blocks - 1):
        chains[k] = product(later_steps[k - 1], chains[k - 1])
    for copy in copies:
        copy.wait()
    for k in range(energies):
        shifts[k] = jnp.full(shifts.shape[1:], held_offsets[group ^ k], jnp.int32)
        first = (group ^ k) * rows
        block = first // (chosen * half)
        tile = held_tiles[block, (first // half) % chosen]
        start = first % half
        row = pl.multiple_of((tile // 2) * half + start, 16)
        column = pl.multiple_of((tile % 2) * half, half)
        mine = slice(k * rows, (k + 1) * rows)
        given[mine] = chains[block, pl.ds(row, rows), :]
        others = slice(energies * rows + k * half, energies * rows + (k + 1) * half)
        given[others] = chains[block, pl.ds(column, half), :]

        def pick(states):
            return jnp.concatenate(
                [
                    states[
                        block,
                        pl.ds(row, rows),
                        pl.ds(pl.multiple_of(column + part * order, half), half),
                    ]
                    for part in range(2)
                ],
                axis=1,
            )

        base, side = parts_at(energies, rows, half, k)

        @pl.when(upper == 0)
        def _():
            own_parts[mine] = pick(lessers)
            given[base : base + rows, side : side + order] = pick(greaters)

        @pl.when(upper == 1)
        def _():
            own_parts[mine] = pick(greaters)
            given[base : base + rows, side : side + order] = pick(lessers)


def tiles_kernel(energies, made, greater, lesser, given, taken, own_parts, pieces, doubled):
    rows, order = pieces[0].shape[1:]
    half = order // 2
    upper = lax.axis_index("domain") & 1

    @pl.when(upper == 0)
    def _():
        doubled[...] = stacked(lesser[...])

    @pl.when(upper == 1)
    def _():
        doubled[...] = stacked(greater[...])

    span = slice(made[0] * rows, (made[-1] + 1) * rows)
    for source, slot in ((given, upper), (taken, 1 - upper)):
        moved = times(source[span], doubled[...]).astype(BF16)
        for i, k in enumerate(made):
            first = energies * rows + k * half
            right = stacked(source[first : first + half])
            if source is given:
                part = own_parts[k * rows : (k + 1) * rows]
            else:
                base, side = parts_at(energies, rows, half, k)
                part = source[base : base + rows, side : side + order]
            pieces[i][slot] = (
                times_adjoint(moved[i * rows : (i + 1) * rows], right) + part.astype(F32)
            ).astype(BF16)


def finish_kernel(energies, made, last, on_last, lesser, greater, *refs):
    operands, refs = refs[:3], refs[3:]
    pieces, doubled = refs[-1 - len(made) : -1], refs[-1]
    at_last = (lax.axis_index("domain") >> 1) == last

    @pl.when(at_last if on_last else jnp.logical_not(at_last))
    def _():
        tiles_kernel(energies, made, greater, lesser, *operands, pieces, doubled)


def finish_own_kernel(energies, last, near, kept, lesser, greater, *refs):
    operands, (piece, doubled, arrived_less, arrived_great) = refs[:3], refs[3:]
    at_last = (lax.axis_index("domain") >> 1) == last

    @pl.when(at_last)
    def _():
        arrived_less[...] = lesser[...]
        arrived_great[...] = greater[...]

    @pl.when(jnp.logical_not(at_last))
    def _():
        arrived_less[...] = near[...]
        arrived_great[...] = kept[...]

    tiles_kernel(
        energies, range(1), arrived_great, arrived_less, *operands, [piece], doubled
    )


def pack_kernel(energies, *refs):
    pieces, out = refs[:energies], refs[energies]
    other = 1 - (lax.axis_index("domain") & 1)
    for k in range(energies):
        out[k] = pieces[k][other]


def convolve_kernel(energies, shifts, swapped, *refs):
    pieces, outs = refs[:energies], refs[energies : 2 * energies]
    upper = lax.axis_index("domain") & 1
    held_less, held_great = refs[2 * energies :]
    group = lax.axis_index("energy")
    rows, width = outs[0].shape
    half = width // 2
    reach = energies // 2

    @pl.when(upper == 0)
    def _():
        for k in range(energies):
            held_less[group ^ k] = pieces[k][0]
            held_great[group ^ k] = swapped[k]

    @pl.when(upper == 1)
    def _():
        for k in range(energies):
            held_less[group ^ k] = swapped[k]
            held_great[group ^ k] = pieces[k][1]

    chunk = 16
    for start in range(0, rows, chunk):
        at = slice(start, start + chunk)
        totals = [None] * energies
        wanted = [jnp.broadcast_to(shifts[k, :1], (chunk, half)) for k in range(energies)]
        for distance in range(-reach, reach + 1):
            real = imag = None
            for e in range(max(0, distance), min(energies, energies + distance)):
                lr = held_less[e, at, :half].astype(F32)
                li = held_less[e, at, half:].astype(F32)
                gr = held_great[e - distance, at, :half].astype(F32)
                gi = held_great[e - distance, at, half:].astype(F32)
                more_real, more_imag = lr * gr - li * gi, lr * gi + li * gr
                real = more_real if real is None else real + more_real
                imag = more_imag if imag is None else imag + more_imag
            for k in range(energies):
                if totals[k] is None:
                    totals[k] = (real, imag)
                else:
                    match = wanted[k] == distance
                    totals[k] = (
                        jnp.where(match, real, totals[k][0]),
                        jnp.where(match, imag, totals[k][1]),
                    )
        for k in range(energies):
            outs[k][at, :half] = (totals[k][0] / energies).astype(BF16)
            outs[k][at, half:] = (totals[k][1] / energies).astype(BF16)


def gather_kernel(energies, *refs):
    shares, (out, sem) = refs[:energies], refs[energies:]
    group = lax.axis_index("energy")
    copies = [
        pltpu.make_async_copy(shares[k], out.at[group ^ k], sem.at[k])
        for k in range(energies)
    ]
    for copy in copies:
        copy.start()
    for copy in copies:
        copy.wait()


def shards(retarded, coupling, sigma_lesser, sigma_greater, tiles, offsets):
    blocks, order = retarded.shape[1], retarded.shape[2]
    half = order // 2
    chosen = tiles.shape[1]
    domains, energies = lax.axis_size("domain"), lax.axis_size("energy")
    chips = domains // 2
    rows = blocks * chosen * half // energies
    unit = 8 * order**3
    block = jax.ShapeDtypeStruct((order, 2 * order), BF16)
    piece = jax.ShapeDtypeStruct((rows, order), BF16)

    def series(count):
        return jax.ShapeDtypeStruct((count, order, 2 * order), BF16)

    def in_place(*arrays):
        return tuple(pltpu.with_memory_space_constraint(x, pltpu.HBM) for x in arrays)

    def swap(x):
        return lax.ppermute(x, "domain", [(d, d ^ 1) for d in range(domains)])

    def hop(x, z, lower=False):
        source, target = 2 * z - 1, 2 * z + (not lower)
        aside = target ^ 1
        if z < chips - 1 or lower or energies % 4:
            ring = [source, target, aside, source - 1]
        else:
            ring = [source, target, source - 1]
        onward = dict(zip(ring, ring[1:] + ring[:1]))
        route = []
        for e in range(energies):
            for d in range(domains):
                if d in onward:
                    place = (e, onward[d])
                elif d == aside:
                    place = (e ^ 2, d)
                else:
                    place = (e, d ^ 1)
                route.append((e * domains + d, place[0] * domains + place[1]))
        return lax.ppermute(x, ("energy", "domain"), route)

    def across(x, k):
        return lax.ppermute(x, "energy", [(e, e ^ k) for e in range(energies)])

    held_retarded, held_coupling, held_less, held_great, *less_set = kernel_call(
        functools.partial(first_kernel, blocks),
        [series(blocks)] * 4 + [series(blocks - 1), series(blocks), block],
        in_place(retarded, coupling, sigma_lesser, sigma_greater),
        (5 * blocks - 3) * unit,
        in_specs=[HBM] * 4,
        scratch=[pltpu.SemaphoreType.DMA((4 * blocks, 2))],
    )
    early_less = less_set[2]
    lower_less = swap(early_less)
    later_steps, less_sources, less_total, *great_set = kernel_call(
        functools.partial(second_kernel, blocks),
        [series(blocks - 1), series(blocks), block]
        + [block, series(blocks), block, block],
        (held_retarded, held_coupling, held_less, held_great, *less_set),
        (5 * blocks - 2) * unit,
        aliases={4: 0, 5: 1},
    )
    early_great, early_whole = great_set[2:]
    (joined_less,) = kernel_call(
        join_first_kernel, [block], (lower_less, early_whole, early_less), 2 * unit
    )
    lower_less = swap(less_total)
    lower_great = swap(early_great)
    first_step, great_sources, great_total, whole = kernel_call(
        functools.partial(third_kernel, blocks),
        [block, series(blocks), block, block],
        (held_retarded, held_coupling, held_great, later_steps, *great_set),
        (5 * blocks - 2) * unit,
        aliases={4: 0, 5: 1},
    )
    (joined_great,) = kernel_call(
        join_first_kernel, [block], (lower_great, early_whole, early_great), 2 * unit
    )
    lower_great = swap(great_total)
    lower_whole = swap(whole)
    chip_great, chip_whole = kernel_call(
        join_kernel,
        [block] * 2,
        (joined_great, lower_great, lower_whole, whole, great_total),
        3 * unit,
    )
    lessers, chip_less = kernel_call(
        functools.partial(prepare_lesser_kernel, blocks),
        [series(blocks), block],
        (whole, joined_less, first_step, later_steps, less_sources, lower_less, less_total),
        4 * unit,
    )
    given, own_parts, shifts = kernel_call(
        functools.partial(prepare_kernel, blocks, energies, chosen),
        [
            jax.ShapeDtypeStruct(
                (energies * (rows + half) + pl.cdiv(energies, 2) * rows, 2 * order), BF16
            ),
            jax.ShapeDtypeStruct((energies * rows, order), BF16),
            jax.ShapeDtypeStruct((energies, 8, half), jnp.int32),
        ],
        (
            *in_place(tiles, offsets),
            first_step,
            later_steps,
            great_sources,
            lower_great,
            great_total,
            chip_great,
            lower_whole,
            whole,
            chip_whole,
            lessers,
        ),
        3 * unit,
        in_specs=[HBM] * 2 + [VMEM] * 10,
        scratch=[pltpu.VMEM((blocks, order, 2 * order), BF16)] * 2
        + [
            pltpu.SMEM(tiles.shape, jnp.int32),
            pltpu.SMEM(offsets.shape, jnp.int32),
            pltpu.SemaphoreType.DMA((2,)),
        ],
    )

    taken = swap(given)

    def step_on(z, state, kept, source):
        return kernel_call(
            functools.partial(advance_kernel, z),
            [block, block],
            (state, chip_whole, source, *kept),
            2 * unit,
        )

    less, great = joined_less, joined_great
    less_in, great_in = (), ()
    for z in range(1, chips):
        less = hop(less, z, lower=z == chips - 1)
        great = hop(great, z)
        if z < chips - 1:
            less, *less_in = step_on(z, less, less_in, chip_less)
            great, *great_in = step_on(z, great, great_in, chip_great)
    if not less_in:
        less_in, great_in = [jnp.zeros_like(less)], [jnp.zeros_like(great)]
    near, kept = swap(*less_in), great_in[0]
    shared = (given, taken, own_parts)
    double = pltpu.VMEM((2 * order, 2 * order), BF16)
    sent = range(1, energies)
    pair = jax.ShapeDtypeStruct((2, rows, order), BF16)
    pieces = ()
    for on_last, arrived in ((False, (near, kept)), (True, (less, great))):
        operands = (*arrived, *shared, *pieces)
        pieces = kernel_call(
            functools.partial(finish_kernel, energies, sent, chips - 1, on_last),
            [pair] * len(sent),
            operands,
            5 * unit,
            scratch=[double],
            aliases={len(operands) - len(pieces) + i: i for i in range(len(pieces))},
        )
    pieces = [across(piece, k) for k, piece in zip(sent, pieces)]
    (own,) = kernel_call(
        functools.partial(finish_own_kernel, energies, chips - 1),
        [pair],
        (near, kept, less, great, *shared),
        2 * unit,
        scratch=[double] + [pltpu.VMEM((order, 2 * order), BF16)] * 2,
    )
    pieces = [own, *pieces]
    (packed,) = kernel_call(
        functools.partial(pack_kernel, energies),
        [jax.ShapeDtypeStruct((energies, rows, order), BF16)],
        pieces,
        0,
    )
    shares = kernel_call(
        functools.partial(convolve_kernel, energies),
        [piece] * energies,
        (shifts, swap(packed), *pieces),
        8 * energies * energies * rows * half,
        scratch=[pltpu.VMEM((energies, rows, order), BF16)] * 2,
    )
    shares = [shares[0]] + [across(shares[k], k) for k in range(1, energies)]
    (result,) = kernel_call(
        functools.partial(gather_kernel, energies),
        [jax.ShapeDtypeStruct((energies, rows, order), BF16)],
        shares,
        0,
        out_specs=[HBM],
        scratch=[pltpu.SemaphoreType.DMA((energies,))],
    )
    return result.reshape(1, blocks, chosen, half, order)


def solution(mesh):
    placed = (
        P("energy", "domain", None, None),
        P("domain", None, None),
        P("energy", "domain", None, None),
        P("energy", "domain", None, None),
        P("domain", None),
        P(),
    )

    return jax.shard_map(
        shards,
        mesh=mesh,
        in_specs=placed,
        out_specs=P("energy", "domain", None, None, None),
        check_vma=False,
    )
```

```python
import functools
import math

import jax
import jax.numpy as jnp
from jax import lax
from jax.experimental import pallas as pl
from jax.experimental.pallas import tpu as pltpu
from jax.sharding import PartitionSpec as P


VMEM_LIMIT = 16 << 20
F32 = jnp.float32
BF16 = jnp.bfloat16
VMEM = pl.BlockSpec(memory_space=pltpu.VMEM)
HBM = pl.BlockSpec(memory_space=pltpu.HBM)


def stacked(block):
    order = block.shape[-1] // 2
    real, imag = block[:, :order], block[:, order:]
    return jnp.concatenate([block, jnp.concatenate([-imag, real], axis=1)], axis=0)


def times(factor, second_stacked):
    return lax.dot_general(
        factor, second_stacked, (((1,), (0,)), ((), ())), preferred_element_type=F32
    )


def times_adjoint(factor, second_stacked):
    return lax.dot_general(
        factor, second_stacked, (((1,), (1,)), ((), ())), preferred_element_type=F32
    )


def product(factor, second):
    return times(factor, stacked(second)).astype(BF16)


def injected(retarded, sigma):
    return times_adjoint(product(retarded, sigma), stacked(retarded)).astype(BF16)


def advance(state, step, source):
    return (times_adjoint(product(step, state), stacked(step)) + source.astype(F32)).astype(
        BF16
    )


def kernel_call(
    body, outs, operands, flops, in_specs=None, scratch=(), out_specs=None, aliases=None
):
    moved = sum(x.size * x.dtype.itemsize for x in operands)
    moved += sum(math.prod(o.shape) * o.dtype.itemsize for o in outs)
    return pl.pallas_call(
        body,
        out_shape=outs,
        in_specs=in_specs or [VMEM] * len(operands),
        out_specs=out_specs or [VMEM] * len(outs),
        scratch_shapes=list(scratch),
        input_output_aliases=aliases or {},
        compiler_params=pltpu.CompilerParams(vmem_limit_bytes=VMEM_LIMIT),
        cost_estimate=pl.CostEstimate(
            flops=int(flops), bytes_accessed=moved, transcendentals=0
        ),
    )(*operands)


class Copies:
    def __init__(self, source, target, sems):
        parts = sems.shape[0]
        rows = target.shape[0] // parts
        self.parts = [
            pltpu.make_async_copy(
                source.at[pl.ds(i * rows, rows)], target.at[pl.ds(i * rows, rows)], sems.at[i]
            )
            for i in range(parts)
        ]
        for part in self.parts:
            part.start()

    def wait(self):
        for part in self.parts:
            part.wait()


def on_first_chip():
    return (lax.axis_index("domain") >> 1) == 0


def lesser_chain(blocks, retarded, coupling, sigma, later_steps, sources, total, ready):
    state = None
    for k in range(blocks):
        ready("r", k)
        ready("l", k)
        source = injected(retarded[k], sigma[k])
        sources[k] = source
        if k > 0:
            ready("c", k)
            step = product(retarded[k], coupling[k])
            later_steps[k - 1] = step
        state = source if k == 0 else advance(state, step, source)
    total[...] = state


def greater_chain(
    blocks, retarded, coupling, sigma, later_steps, first_step, sources, total, whole
):
    state = chain = None
    for k in range(blocks):
        source = injected(retarded[k], sigma[k])
        sources[k] = source
        if k == 0:
            chain = product(retarded[0], coupling[0])
            first_step[...] = chain
            state = source
        else:
            step = later_steps[k - 1]
            chain = product(step, chain)
            state = advance(state, step, source)
    total[...] = state
    whole[...] = chain


def first_kernel(
    blocks,
    retarded,
    coupling,
    lesser,
    greater,
    held_retarded,
    held_coupling,
    held_lesser,
    held_greater,
    later_steps,
    sources,
    total,
    sem,
):
    copies = {}
    for k in range(blocks):
        copies["r", k] = (retarded.at[0, k], held_retarded.at[k])
        copies["l", k] = (lesser.at[0, k], held_lesser.at[k])
        if k > 0:
            copies["c", k] = (coupling.at[k], held_coupling.at[k])
    copies["c", 0] = (coupling.at[0], held_coupling.at[0])
    for k in range(blocks):
        copies["g", k] = (greater.at[0, k], held_greater.at[k])
    for index, (key, (source, target)) in enumerate(copies.items()):
        copies[key] = Copies(source, target, sem.at[index])
    early = [key for key in copies if key[0] in "rl" or (key[0] == "c" and key[1] > 0)]
    first_chip = on_first_chip()

    @pl.when(first_chip)
    def _():
        lesser_chain(
            blocks,
            held_retarded,
            held_coupling,
            held_lesser,
            later_steps,
            sources,
            total,
            lambda *key: copies[key].wait(),
        )

    @pl.when(jnp.logical_not(first_chip))
    def _():
        for key in early:
            copies[key].wait()

    for key in copies:
        if key not in early:
            copies[key].wait()


def second_kernel(
    blocks,
    retarded,
    coupling,
    lesser,
    greater,
    given_steps,
    given_sources,
    given_total,
    later_steps,
    less_sources,
    less_total,
    first_step,
    great_sources,
    great_total,
    whole,
):
    first_chip = on_first_chip()

    @pl.when(first_chip)
    def _():
        greater_chain(
            blocks,
            retarded,
            coupling,
            greater,
            given_steps,
            first_step,
            great_sources,
            great_total,
            whole,
        )
        less_total[...] = given_total[...]

    @pl.when(jnp.logical_not(first_chip))
    def _():
        lesser_chain(
            blocks,
            retarded,
            coupling,
            lesser,
            later_steps,
            less_sources,
            less_total,
            lambda *key: None,
        )


def third_kernel(
    blocks,
    retarded,
    coupling,
    greater,
    later_steps,
    given_step,
    given_sources,
    given_total,
    given_whole,
    first_step,
    sources,
    total,
    whole,
):
    first_chip = on_first_chip()

    @pl.when(first_chip)
    def _():
        total[...] = given_total[...]
        whole[...] = given_whole[...]

    @pl.when(jnp.logical_not(first_chip))
    def _():
        greater_chain(
            blocks,
            retarded,
            coupling,
            greater,
            later_steps,
            first_step,
            sources,
            total,
            whole,
        )


def join_first_kernel(lower, whole, upper, out):
    @pl.when(lax.axis_index("domain") == 1)
    def _():
        out[...] = advance(lower[...], whole[...], upper[...])


def join_kernel(joined, lower, whole, upper, chip):
    on_upper = (lax.axis_index("domain") & 1) == 1
    first_chip = on_first_chip()

    @pl.when(on_upper & first_chip)
    def _():
        chip[...] = joined[...]

    @pl.when(on_upper & jnp.logical_not(first_chip))
    def _():
        chip[...] = advance(lower[...], whole[...], upper[...])


def join_whole_kernel(whole, lower_whole, chip_whole):
    @pl.when((lax.axis_index("domain") & 1) == 1)
    def _():
        chip_whole[...] = product(whole[...], lower_whole[...])


def keep(z, state, kept, out):
    chip = lax.axis_index("domain") >> 1

    @pl.when(chip == z)
    def _():
        out[...] = state[...]

    @pl.when(chip != z)
    def _():
        out[...] = jnp.zeros_like(out) if kept is None else kept[...]


def advance_kernel(z, state, step, source, *refs):
    kept, (out, chosen) = (refs[0] if len(refs) == 3 else None), refs[-2:]

    @pl.when((lax.axis_index("domain") >> 1) == z)
    def _():
        out[...] = advance(state[...], step[...], source[...])

    keep(z, state, kept, chosen)


def parts_at(energies, rows, half, k):
    below = energies * (rows + half)
    return below + (k // 2) * rows, (k % 2) * 2 * half


def states_of(blocks, first_step, later_steps, sources, lower, total, chip, states):
    upper = lax.axis_index("domain") & 1

    @pl.when(upper == 0)
    def _():
        states[0] = sources[0]
        if blocks > 1:
            states[blocks - 1] = total[...]

    @pl.when(upper == 1)
    def _():
        if blocks > 1:
            states[0] = advance(lower[...], first_step[...], sources[0])
        states[blocks - 1] = chip[...]

    for k in range(1, blocks - 1):
        states[k] = advance(states[k - 1], later_steps[k - 1], sources[k])


def prepare_kernel(
    blocks,
    energies,
    chosen,
    tiles,
    offsets,
    first_step,
    later_steps,
    lesser_sources,
    lower_less,
    less_total,
    chip_less,
    greater_sources,
    lower_great,
    great_total,
    chip_great,
    lower_whole,
    whole,
    chip_whole,
    given,
    own_parts,
    shifts,
    chains,
    lessers,
    greaters,
    held_tiles,
    held_offsets,
    sem,
):
    copies = [
        pltpu.make_async_copy(tiles, held_tiles, sem.at[0]),
        pltpu.make_async_copy(offsets, held_offsets, sem.at[1]),
    ]
    for copy in copies:
        copy.start()
    upper = lax.axis_index("domain") & 1
    group = lax.axis_index("energy")
    order = first_step.shape[0]
    half = order // 2
    rows = blocks * chosen * half // energies
    for sources, lower, total, chip, states in (
        (lesser_sources, lower_less, less_total, chip_less, lessers),
        (greater_sources, lower_great, great_total, chip_great, greaters),
    ):
        states_of(blocks, first_step, later_steps, sources, lower, total, chip, states)

    @pl.when(upper == 0)
    def _():
        chains[0] = first_step[...]
        chains[blocks - 1] = whole[...]

    @pl.when(upper == 1)
    def _():
        if blocks > 1:
            chains[0] = product(first_step[...], lower_whole[...])
        chains[blocks - 1] = chip_whole[...]

    for k in range(1, blocks - 1):
        chains[k] = product(later_steps[k - 1], chains[k - 1])
    for copy in copies:
        copy.wait()
    for k in range(energies):
        shifts[k] = jnp.full(shifts.shape[1:], held_offsets[group ^ k], jnp.int32)
        first = (group ^ k) * rows
        block = first // (chosen * half)
        tile = held_tiles[block, (first // half) % chosen]
        start = first % half
        row = pl.multiple_of((tile // 2) * half + start, 16)
        column = pl.multiple_of((tile % 2) * half, half)
        mine = slice(k * rows, (k + 1) * rows)
        given[mine] = chains[block, pl.ds(row, rows), :]
        others = slice(energies * rows + k * half, energies * rows + (k + 1) * half)
        given[others] = chains[block, pl.ds(column, half), :]

        def pick(states):
            return jnp.concatenate(
                [
                    states[
                        block,
                        pl.ds(row, rows),
                        pl.ds(pl.multiple_of(column + part * order, half), half),
                    ]
                    for part in range(2)
                ],
                axis=1,
            )

        base, side = parts_at(energies, rows, half, k)

        @pl.when(upper == 0)
        def _():
            own_parts[mine] = pick(lessers)
            given[base : base + rows, side : side + order] = pick(greaters)

        @pl.when(upper == 1)
        def _():
            own_parts[mine] = pick(greaters)
            given[base : base + rows, side : side + order] = pick(lessers)


def tiles_kernel(energies, made, greater, lesser, given, taken, own_parts, pieces, doubled):
    rows, order = pieces[0].shape[1:]
    half = order // 2
    upper = lax.axis_index("domain") & 1

    @pl.when(upper == 0)
    def _():
        doubled[...] = stacked(lesser[...])

    @pl.when(upper == 1)
    def _():
        doubled[...] = stacked(greater[...])

    span = slice(made[0] * rows, (made[-1] + 1) * rows)
    for source, slot in ((given, upper), (taken, 1 - upper)):
        moved = times(source[span], doubled[...]).astype(BF16)
        for i, k in enumerate(made):
            first = energies * rows + k * half
            right = stacked(source[first : first + half])
            if source is given:
                part = own_parts[k * rows : (k + 1) * rows]
            else:
                base, side = parts_at(energies, rows, half, k)
                part = source[base : base + rows, side : side + order]
            pieces[i][slot] = (
                times_adjoint(moved[i * rows : (i + 1) * rows], right) + part.astype(F32)
            ).astype(BF16)


def finish_kernel(energies, made, last, on_last, lesser, greater, *refs):
    operands, refs = refs[:3], refs[3:]
    pieces, doubled = refs[-1 - len(made) : -1], refs[-1]
    at_last = (lax.axis_index("domain") >> 1) == last

    @pl.when(at_last if on_last else jnp.logical_not(at_last))
    def _():
        tiles_kernel(energies, made, greater, lesser, *operands, pieces, doubled)


def finish_own_kernel(energies, last, near, kept, lesser, greater, *refs):
    operands, (piece, doubled, arrived_less, arrived_great) = refs[:3], refs[3:]
    at_last = (lax.axis_index("domain") >> 1) == last

    @pl.when(at_last)
    def _():
        arrived_less[...] = lesser[...]
        arrived_great[...] = greater[...]

    @pl.when(jnp.logical_not(at_last))
    def _():
        arrived_less[...] = near[...]
        arrived_great[...] = kept[...]

    tiles_kernel(
        energies, range(1), arrived_great, arrived_less, *operands, [piece], doubled
    )


def pack_kernel(energies, *refs):
    pieces, out = refs[:energies], refs[energies]
    other = 1 - (lax.axis_index("domain") & 1)
    for k in range(energies):
        out[k] = pieces[k][other]


def convolve_kernel(energies, shifts, swapped, *refs):
    pieces, outs = refs[:energies], refs[energies : 2 * energies]
    upper = lax.axis_index("domain") & 1
    held_less, held_great = refs[2 * energies :]
    group = lax.axis_index("energy")
    rows, width = outs[0].shape
    half = width // 2
    reach = energies // 2

    @pl.when(upper == 0)
    def _():
        for k in range(energies):
            held_less[group ^ k] = pieces[k][0]
            held_great[group ^ k] = swapped[k]

    @pl.when(upper == 1)
    def _():
        for k in range(energies):
            held_less[group ^ k] = swapped[k]
            held_great[group ^ k] = pieces[k][1]

    chunk = 16
    for start in range(0, rows, chunk):
        at = slice(start, start + chunk)
        totals = [None] * energies
        wanted = [jnp.broadcast_to(shifts[k, :1], (chunk, half)) for k in range(energies)]
        for distance in range(-reach, reach + 1):
            real = imag = None
            for e in range(max(0, distance), min(energies, energies + distance)):
                lr = held_less[e, at, :half].astype(F32)
                li = held_less[e, at, half:].astype(F32)
                gr = held_great[e - distance, at, :half].astype(F32)
                gi = held_great[e - distance, at, half:].astype(F32)
                more_real, more_imag = lr * gr - li * gi, lr * gi + li * gr
                real = more_real if real is None else real + more_real
                imag = more_imag if imag is None else imag + more_imag
            for k in range(energies):
                if totals[k] is None:
                    totals[k] = (real, imag)
                else:
                    match = wanted[k] == distance
                    totals[k] = (
                        jnp.where(match, real, totals[k][0]),
                        jnp.where(match, imag, totals[k][1]),
                    )
        for k in range(energies):
            outs[k][at, :half] = (totals[k][0] / energies).astype(BF16)
            outs[k][at, half:] = (totals[k][1] / energies).astype(BF16)


def gather_kernel(energies, *refs):
    shares, (out, sem) = refs[:energies], refs[energies:]
    group = lax.axis_index("energy")
    copies = [
        pltpu.make_async_copy(shares[k], out.at[group ^ k], sem.at[k])
        for k in range(energies)
    ]
    for copy in copies:
        copy.start()
    for copy in copies:
        copy.wait()


def shards(retarded, coupling, sigma_lesser, sigma_greater, tiles, offsets):
    blocks, order = retarded.shape[1], retarded.shape[2]
    half = order // 2
    chosen = tiles.shape[1]
    domains, energies = lax.axis_size("domain"), lax.axis_size("energy")
    chips = domains // 2
    rows = blocks * chosen * half // energies
    unit = 8 * order**3
    block = jax.ShapeDtypeStruct((order, 2 * order), BF16)
    piece = jax.ShapeDtypeStruct((rows, order), BF16)

    def series(count):
        return jax.ShapeDtypeStruct((count, order, 2 * order), BF16)

    def in_place(*arrays):
        return tuple(pltpu.with_memory_space_constraint(x, pltpu.HBM) for x in arrays)

    def swap(x):
        return lax.ppermute(x, "domain", [(d, d ^ 1) for d in range(domains)])

    def hop(x, z, lower=False):
        source, target = 2 * z - 1, 2 * z + (not lower)
        before, aside = source - 1, target ^ 1
        if energies % 4 or lower or z == 1 < chips - 1:
            ring = [source, target, aside, before]
        elif z < chips - 1:
            ring = [source, target]
        else:
            ring = [source, target, before]
        onward = dict(zip(ring, ring[1:] + ring[:1]))
        route = []
        for e in range(energies):
            for d in range(domains):
                if d in onward:
                    place = (e, onward[d])
                elif d in (before, aside):
                    place = (e ^ 2, d)
                else:
                    place = (e, d ^ 1)
                route.append((e * domains + d, place[0] * domains + place[1]))
        return lax.ppermute(x, ("energy", "domain"), route)

    def across(x, k):
        return lax.ppermute(x, "energy", [(e, e ^ k) for e in range(energies)])

    held_retarded, held_coupling, held_less, held_great, *less_set = kernel_call(
        functools.partial(first_kernel, blocks),
        [series(blocks)] * 4 + [series(blocks - 1), series(blocks), block],
        in_place(retarded, coupling, sigma_lesser, sigma_greater),
        (5 * blocks - 3) * unit,
        in_specs=[HBM] * 4,
        scratch=[pltpu.SemaphoreType.DMA((4 * blocks, 2))],
    )
    early_less = less_set[2]
    lower_less = swap(early_less)
    later_steps, less_sources, less_total, *great_set = kernel_call(
        functools.partial(second_kernel, blocks),
        [series(blocks - 1), series(blocks), block]
        + [block, series(blocks), block, block],
        (held_retarded, held_coupling, held_less, held_great, *less_set),
        (5 * blocks - 2) * unit,
        aliases={4: 0, 5: 1},
    )
    early_great, early_whole = great_set[2:]
    (joined_less,) = kernel_call(
        join_first_kernel, [block], (lower_less, early_whole, early_less), 2 * unit
    )
    lower_less = swap(less_total)
    lower_great = swap(early_great)
    first_step, great_sources, great_total, whole = kernel_call(
        functools.partial(third_kernel, blocks),
        [block, series(blocks), block, block],
        (held_retarded, held_coupling, held_great, later_steps, *great_set),
        (5 * blocks - 2) * unit,
        aliases={4: 0, 5: 1},
    )
    (joined_great,) = kernel_call(
        join_first_kernel, [block], (lower_great, early_whole, early_great), 2 * unit
    )
    lower_great = swap(great_total)
    lower_whole = swap(whole)
    (chip_less,) = kernel_call(
        join_kernel, [block], (joined_less, lower_less, whole, less_total), 2 * unit
    )
    (chip_whole,) = kernel_call(join_whole_kernel, [block], (whole, lower_whole), unit)
    (chip_great,) = kernel_call(
        join_kernel, [block], (joined_great, lower_great, whole, great_total), 2 * unit
    )
    given, own_parts, shifts = kernel_call(
        functools.partial(prepare_kernel, blocks, energies, chosen),
        [
            jax.ShapeDtypeStruct(
                (energies * (rows + half) + pl.cdiv(energies, 2) * rows, 2 * order), BF16
            ),
            jax.ShapeDtypeStruct((energies * rows, order), BF16),
            jax.ShapeDtypeStruct((energies, 8, half), jnp.int32),
        ],
        (
            *in_place(tiles, offsets),
            first_step,
            later_steps,
            less_sources,
            lower_less,
            less_total,
            chip_less,
            great_sources,
            lower_great,
            great_total,
            chip_great,
            lower_whole,
            whole,
            chip_whole,
        ),
        5 * unit,
        in_specs=[HBM] * 2 + [VMEM] * 13,
        scratch=[pltpu.VMEM((blocks, order, 2 * order), BF16)] * 3
        + [
            pltpu.SMEM(tiles.shape, jnp.int32),
            pltpu.SMEM(offsets.shape, jnp.int32),
            pltpu.SemaphoreType.DMA((2,)),
        ],
    )

    taken = swap(given)

    def step_on(z, state, kept, source):
        return kernel_call(
            functools.partial(advance_kernel, z),
            [block, block],
            (state, chip_whole, source, *kept),
            2 * unit,
        )

    less, great = joined_less, joined_great
    less_in, great_in = (), ()
    for z in range(1, chips):
        less = hop(less, z, lower=z == chips - 1)
        great = hop(great, z)
        if z < chips - 1:
            less, *less_in = step_on(z, less, less_in, chip_less)
            great, *great_in = step_on(z, great, great_in, chip_great)
    if not less_in:
        less_in, great_in = [jnp.zeros_like(less)], [jnp.zeros_like(great)]
    near, kept = swap(*less_in), great_in[0]
    shared = (given, taken, own_parts)
    double = pltpu.VMEM((2 * order, 2 * order), BF16)
    sent = range(1, energies)
    pair = jax.ShapeDtypeStruct((2, rows, order), BF16)
    pieces = ()
    for on_last, arrived in ((False, (near, kept)), (True, (less, great))):
        operands = (*arrived, *shared, *pieces)
        pieces = kernel_call(
            functools.partial(finish_kernel, energies, sent, chips - 1, on_last),
            [pair] * len(sent),
            operands,
            5 * unit,
            scratch=[double],
            aliases={len(operands) - len(pieces) + i: i for i in range(len(pieces))},
        )
    pieces = [across(piece, k) for k, piece in zip(sent, pieces)]
    (own,) = kernel_call(
        functools.partial(finish_own_kernel, energies, chips - 1),
        [pair],
        (near, kept, less, great, *shared),
        2 * unit,
        scratch=[double] + [pltpu.VMEM((order, 2 * order), BF16)] * 2,
    )
    pieces = [own, *pieces]
    (packed,) = kernel_call(
        functools.partial(pack_kernel, energies),
        [jax.ShapeDtypeStruct((energies, rows, order), BF16)],
        pieces,
        0,
    )
    shares = kernel_call(
        functools.partial(convolve_kernel, energies),
        [piece] * energies,
        (shifts, swap(packed), *pieces),
        8 * energies * energies * rows * half,
        scratch=[pltpu.VMEM((energies, rows, order), BF16)] * 2,
    )
    shares = [shares[0]] + [across(shares[k], k) for k in range(1, energies)]
    (result,) = kernel_call(
        functools.partial(gather_kernel, energies),
        [jax.ShapeDtypeStruct((energies, rows, order), BF16)],
        shares,
        0,
        out_specs=[HBM],
        scratch=[pltpu.SemaphoreType.DMA((energies,))],
    )
    return result.reshape(1, blocks, chosen, half, order)


def solution(mesh):
    placed = (
        P("energy", "domain", None, None),
        P("domain", None, None),
        P("energy", "domain", None, None),
        P("energy", "domain", None, None),
        P("domain", None),
        P(),
    )

    return jax.shard_map(
        shards,
        mesh=mesh,
        in_specs=placed,
        out_specs=P("energy", "domain", None, None, None),
        check_vma=False,
    )
```

```python
import functools
import math

import jax
import jax.numpy as jnp
from jax import lax
from jax.experimental import pallas as pl
from jax.experimental.pallas import tpu as pltpu
from jax.sharding import PartitionSpec as P


VMEM_LIMIT = 16 << 20
F32 = jnp.float32
BF16 = jnp.bfloat16
VMEM = pl.BlockSpec(memory_space=pltpu.VMEM)
HBM = pl.BlockSpec(memory_space=pltpu.HBM)


def stacked(block):
    order = block.shape[-1] // 2
    real, imag = block[:, :order], block[:, order:]
    return jnp.concatenate([block, jnp.concatenate([-imag, real], axis=1)], axis=0)


def times(factor, second_stacked):
    return lax.dot_general(
        factor, second_stacked, (((1,), (0,)), ((), ())), preferred_element_type=F32
    )


def times_adjoint(factor, second_stacked):
    return lax.dot_general(
        factor, second_stacked, (((1,), (1,)), ((), ())), preferred_element_type=F32
    )


def product(factor, second):
    return times(factor, stacked(second)).astype(BF16)


def injected(retarded, sigma):
    return times_adjoint(product(retarded, sigma), stacked(retarded)).astype(BF16)


def advance(state, step, source):
    return (times_adjoint(product(step, state), stacked(step)) + source.astype(F32)).astype(
        BF16
    )


def kernel_call(
    body, outs, operands, flops, in_specs=None, scratch=(), out_specs=None, aliases=None
):
    moved = sum(x.size * x.dtype.itemsize for x in operands)
    moved += sum(math.prod(o.shape) * o.dtype.itemsize for o in outs)
    return pl.pallas_call(
        body,
        out_shape=outs,
        in_specs=in_specs or [VMEM] * len(operands),
        out_specs=out_specs or [VMEM] * len(outs),
        scratch_shapes=list(scratch),
        input_output_aliases=aliases or {},
        compiler_params=pltpu.CompilerParams(vmem_limit_bytes=VMEM_LIMIT),
        cost_estimate=pl.CostEstimate(
            flops=int(flops), bytes_accessed=moved, transcendentals=0
        ),
    )(*operands)


class Copies:
    def __init__(self, source, target, sems):
        parts = sems.shape[0]
        rows = target.shape[0] // parts
        self.parts = [
            pltpu.make_async_copy(
                source.at[pl.ds(i * rows, rows)], target.at[pl.ds(i * rows, rows)], sems.at[i]
            )
            for i in range(parts)
        ]
        for part in self.parts:
            part.start()

    def wait(self):
        for part in self.parts:
            part.wait()


def on_first_chip():
    return (lax.axis_index("domain") >> 1) == 0


def lesser_chain(blocks, retarded, coupling, sigma, later_steps, sources, total, ready):
    state = None
    for k in range(blocks):
        ready("r", k)
        ready("l", k)
        source = injected(retarded[k], sigma[k])
        sources[k] = source
        if k > 0:
            ready("c", k)
            step = product(retarded[k], coupling[k])
            later_steps[k - 1] = step
        state = source if k == 0 else advance(state, step, source)
    total[...] = state


def greater_chain(
    blocks, retarded, coupling, sigma, later_steps, first_step, sources, total, whole
):
    state = chain = None
    for k in range(blocks):
        source = injected(retarded[k], sigma[k])
        sources[k] = source
        if k == 0:
            chain = product(retarded[0], coupling[0])
            first_step[...] = chain
            state = source
        else:
            step = later_steps[k - 1]
            chain = product(step, chain)
            state = advance(state, step, source)
    total[...] = state
    whole[...] = chain


def first_kernel(
    blocks,
    retarded,
    coupling,
    lesser,
    greater,
    held_retarded,
    held_coupling,
    held_lesser,
    held_greater,
    later_steps,
    sources,
    total,
    sem,
):
    copies = {}
    for k in range(blocks):
        copies["r", k] = (retarded.at[0, k], held_retarded.at[k])
        copies["l", k] = (lesser.at[0, k], held_lesser.at[k])
        if k > 0:
            copies["c", k] = (coupling.at[k], held_coupling.at[k])
    copies["c", 0] = (coupling.at[0], held_coupling.at[0])
    for k in range(blocks):
        copies["g", k] = (greater.at[0, k], held_greater.at[k])
    for index, (key, (source, target)) in enumerate(copies.items()):
        copies[key] = Copies(source, target, sem.at[index])
    early = [key for key in copies if key[0] in "rl" or (key[0] == "c" and key[1] > 0)]
    first_chip = on_first_chip()

    @pl.when(first_chip)
    def _():
        lesser_chain(
            blocks,
            held_retarded,
            held_coupling,
            held_lesser,
            later_steps,
            sources,
            total,
            lambda *key: copies[key].wait(),
        )

    @pl.when(jnp.logical_not(first_chip))
    def _():
        for key in early:
            copies[key].wait()

    for key in copies:
        if key not in early:
            copies[key].wait()


def second_kernel(
    blocks,
    retarded,
    coupling,
    lesser,
    greater,
    given_steps,
    given_sources,
    given_total,
    later_steps,
    less_sources,
    less_total,
    first_step,
    great_sources,
    great_total,
    whole,
):
    first_chip = on_first_chip()

    @pl.when(first_chip)
    def _():
        greater_chain(
            blocks,
            retarded,
            coupling,
            greater,
            given_steps,
            first_step,
            great_sources,
            great_total,
            whole,
        )
        less_total[...] = given_total[...]

    @pl.when(jnp.logical_not(first_chip))
    def _():
        lesser_chain(
            blocks,
            retarded,
            coupling,
            lesser,
            later_steps,
            less_sources,
            less_total,
            lambda *key: None,
        )


def third_kernel(
    blocks,
    retarded,
    coupling,
    greater,
    later_steps,
    given_step,
    given_sources,
    given_total,
    given_whole,
    first_step,
    sources,
    total,
    whole,
):
    first_chip = on_first_chip()

    @pl.when(first_chip)
    def _():
        total[...] = given_total[...]
        whole[...] = given_whole[...]

    @pl.when(jnp.logical_not(first_chip))
    def _():
        greater_chain(
            blocks,
            retarded,
            coupling,
            greater,
            later_steps,
            first_step,
            sources,
            total,
            whole,
        )


def join_first_kernel(lower, whole, upper, out):
    @pl.when(lax.axis_index("domain") == 1)
    def _():
        out[...] = advance(lower[...], whole[...], upper[...])


def join_kernel(joined, lower, whole, upper, chip):
    on_upper = (lax.axis_index("domain") & 1) == 1
    first_chip = on_first_chip()

    @pl.when(on_upper & first_chip)
    def _():
        chip[...] = joined[...]

    @pl.when(on_upper & jnp.logical_not(first_chip))
    def _():
        chip[...] = advance(lower[...], whole[...], upper[...])


def join_whole_kernel(whole, lower_whole, chip_whole):
    @pl.when((lax.axis_index("domain") & 1) == 1)
    def _():
        chip_whole[...] = product(whole[...], lower_whole[...])


def keep(z, state, kept, out):
    chip = lax.axis_index("domain") >> 1

    @pl.when(chip == z)
    def _():
        out[...] = state[...]

    @pl.when(chip != z)
    def _():
        out[...] = jnp.zeros_like(out) if kept is None else kept[...]


def advance_kernel(z, state, step, source, *refs):
    kept, (out, chosen) = (refs[0] if len(refs) == 3 else None), refs[-2:]

    @pl.when(lax.axis_index("domain") == 2 * z + 1)
    def _():
        out[...] = advance(state[...], step[...], source[...])

    keep(z, state, kept, chosen)


def parts_at(energies, rows, half, k):
    below = energies * (rows + half)
    return below + (k // 2) * rows, (k % 2) * 2 * half


def states_of(blocks, first_step, later_steps, sources, lower, total, chip, states):
    upper = lax.axis_index("domain") & 1

    @pl.when(upper == 0)
    def _():
        states[0] = sources[0]
        if blocks > 1:
            states[blocks - 1] = total[...]

    @pl.when(upper == 1)
    def _():
        if blocks > 1:
            states[0] = advance(lower[...], first_step[...], sources[0])
        states[blocks - 1] = chip[...]

    for k in range(1, blocks - 1):
        states[k] = advance(states[k - 1], later_steps[k - 1], sources[k])


def prepare_kernel(
    blocks,
    energies,
    chosen,
    tiles,
    offsets,
    first_step,
    later_steps,
    lesser_sources,
    lower_less,
    less_total,
    chip_less,
    greater_sources,
    lower_great,
    great_total,
    chip_great,
    lower_whole,
    whole,
    chip_whole,
    given,
    own_parts,
    shifts,
    chains,
    lessers,
    greaters,
    held_tiles,
    held_offsets,
    sem,
):
    copies = [
        pltpu.make_async_copy(tiles, held_tiles, sem.at[0]),
        pltpu.make_async_copy(offsets, held_offsets, sem.at[1]),
    ]
    for copy in copies:
        copy.start()
    upper = lax.axis_index("domain") & 1
    group = lax.axis_index("energy")
    order = first_step.shape[0]
    half = order // 2
    rows = blocks * chosen * half // energies
    for sources, lower, total, chip, states in (
        (lesser_sources, lower_less, less_total, chip_less, lessers),
        (greater_sources, lower_great, great_total, chip_great, greaters),
    ):
        states_of(blocks, first_step, later_steps, sources, lower, total, chip, states)

    @pl.when(upper == 0)
    def _():
        chains[0] = first_step[...]
        chains[blocks - 1] = whole[...]

    @pl.when(upper == 1)
    def _():
        if blocks > 1:
            chains[0] = product(first_step[...], lower_whole[...])
        chains[blocks - 1] = chip_whole[...]

    for k in range(1, blocks - 1):
        chains[k] = product(later_steps[k - 1], chains[k - 1])
    for copy in copies:
        copy.wait()
    for k in range(energies):
        shifts[k] = jnp.full(shifts.shape[1:], held_offsets[group ^ k], jnp.int32)
        first = (group ^ k) * rows
        block = first // (chosen * half)
        tile = held_tiles[block, (first // half) % chosen]
        start = first % half
        row = pl.multiple_of((tile // 2) * half + start, 16)
        column = pl.multiple_of((tile % 2) * half, half)
        mine = slice(k * rows, (k + 1) * rows)
        given[mine] = chains[block, pl.ds(row, rows), :]
        others = slice(energies * rows + k * half, energies * rows + (k + 1) * half)
        given[others] = chains[block, pl.ds(column, half), :]

        def pick(states):
            return jnp.concatenate(
                [
                    states[
                        block,
                        pl.ds(row, rows),
                        pl.ds(pl.multiple_of(column + part * order, half), half),
                    ]
                    for part in range(2)
                ],
                axis=1,
            )

        base, side = parts_at(energies, rows, half, k)

        @pl.when(upper == 0)
        def _():
            own_parts[mine] = pick(lessers)
            given[base : base + rows, side : side + order] = pick(greaters)

        @pl.when(upper == 1)
        def _():
            own_parts[mine] = pick(greaters)
            given[base : base + rows, side : side + order] = pick(lessers)


def tiles_kernel(energies, made, greater, lesser, given, taken, own_parts, pieces, doubled):
    rows, order = pieces[0].shape[1:]
    half = order // 2
    upper = lax.axis_index("domain") & 1

    @pl.when(upper == 0)
    def _():
        doubled[...] = stacked(lesser[...])

    @pl.when(upper == 1)
    def _():
        doubled[...] = stacked(greater[...])

    span = slice(made[0] * rows, (made[-1] + 1) * rows)
    for source, slot in ((given, upper), (taken, 1 - upper)):
        moved = times(source[span], doubled[...]).astype(BF16)
        for i, k in enumerate(made):
            first = energies * rows + k * half
            right = stacked(source[first : first + half])
            if source is given:
                part = own_parts[k * rows : (k + 1) * rows]
            else:
                base, side = parts_at(energies, rows, half, k)
                part = source[base : base + rows, side : side + order]
            pieces[i][slot] = (
                times_adjoint(moved[i * rows : (i + 1) * rows], right) + part.astype(F32)
            ).astype(BF16)


def finish_kernel(energies, made, last, on_last, lesser, greater, *refs):
    operands, refs = refs[:3], refs[3:]
    pieces, doubled = refs[-1 - len(made) : -1], refs[-1]
    at_last = (lax.axis_index("domain") >> 1) == last

    @pl.when(at_last if on_last else jnp.logical_not(at_last))
    def _():
        tiles_kernel(energies, made, greater, lesser, *operands, pieces, doubled)


def finish_own_kernel(energies, last, near, kept, lesser, greater, *refs):
    operands, (piece, doubled, arrived_less, arrived_great) = refs[:3], refs[3:]
    at_last = (lax.axis_index("domain") >> 1) == last

    @pl.when(at_last)
    def _():
        arrived_less[...] = lesser[...]
        arrived_great[...] = greater[...]

    @pl.when(jnp.logical_not(at_last))
    def _():
        arrived_less[...] = near[...]
        arrived_great[...] = kept[...]

    tiles_kernel(
        energies, range(1), arrived_great, arrived_less, *operands, [piece], doubled
    )


def pack_kernel(energies, *refs):
    pieces, out = refs[:energies], refs[energies]
    other = 1 - (lax.axis_index("domain") & 1)
    for k in range(energies):
        out[k] = pieces[k][other]


def convolve_kernel(energies, shifts, swapped, *refs):
    pieces, outs = refs[:energies], refs[energies : 2 * energies]
    upper = lax.axis_index("domain") & 1
    held_less, held_great = refs[2 * energies :]
    group = lax.axis_index("energy")
    rows, width = outs[0].shape
    half = width // 2
    reach = energies // 2

    @pl.when(upper == 0)
    def _():
        for k in range(energies):
            held_less[group ^ k] = pieces[k][0]
            held_great[group ^ k] = swapped[k]

    @pl.when(upper == 1)
    def _():
        for k in range(energies):
            held_less[group ^ k] = swapped[k]
            held_great[group ^ k] = pieces[k][1]

    chunk = 16
    for start in range(0, rows, chunk):
        at = slice(start, start + chunk)
        totals = [None] * energies
        wanted = [jnp.broadcast_to(shifts[k, :1], (chunk, half)) for k in range(energies)]
        for distance in range(-reach, reach + 1):
            real = imag = None
            for e in range(max(0, distance), min(energies, energies + distance)):
                lr = held_less[e, at, :half].astype(F32)
                li = held_less[e, at, half:].astype(F32)
                gr = held_great[e - distance, at, :half].astype(F32)
                gi = held_great[e - distance, at, half:].astype(F32)
                more_real, more_imag = lr * gr - li * gi, lr * gi + li * gr
                real = more_real if real is None else real + more_real
                imag = more_imag if imag is None else imag + more_imag
            for k in range(energies):
                if totals[k] is None:
                    totals[k] = (real, imag)
                else:
                    match = wanted[k] == distance
                    totals[k] = (
                        jnp.where(match, real, totals[k][0]),
                        jnp.where(match, imag, totals[k][1]),
                    )
        for k in range(energies):
            outs[k][at, :half] = (totals[k][0] / energies).astype(BF16)
            outs[k][at, half:] = (totals[k][1] / energies).astype(BF16)


def gather_kernel(energies, *refs):
    shares, (out, sem) = refs[:energies], refs[energies:]
    group = lax.axis_index("energy")
    copies = [
        pltpu.make_async_copy(shares[k], out.at[group ^ k], sem.at[k])
        for k in range(energies)
    ]
    for copy in copies:
        copy.start()
    for copy in copies:
        copy.wait()


def shards(retarded, coupling, sigma_lesser, sigma_greater, tiles, offsets):
    blocks, order = retarded.shape[1], retarded.shape[2]
    half = order // 2
    chosen = tiles.shape[1]
    domains, energies = lax.axis_size("domain"), lax.axis_size("energy")
    chips = domains // 2
    rows = blocks * chosen * half // energies
    unit = 8 * order**3
    block = jax.ShapeDtypeStruct((order, 2 * order), BF16)
    piece = jax.ShapeDtypeStruct((rows, order), BF16)

    def series(count):
        return jax.ShapeDtypeStruct((count, order, 2 * order), BF16)

    def in_place(*arrays):
        return tuple(pltpu.with_memory_space_constraint(x, pltpu.HBM) for x in arrays)

    def swap(x):
        return lax.ppermute(x, "domain", [(d, d ^ 1) for d in range(domains)])

    def hop(x, z, lower=False):
        source, target = 2 * z - 1, 2 * z + (not lower)
        before, aside = source - 1, target ^ 1
        if energies % 4 or lower or z < chips - 1:
            ring = [source, target, aside, before]
        else:
            ring = [source, target, before]
        onward = dict(zip(ring, ring[1:] + ring[:1]))
        route = []
        for e in range(energies):
            for d in range(domains):
                if d in onward:
                    place = (e, onward[d])
                elif d == aside:
                    place = (e ^ 2, d)
                else:
                    place = (e, d ^ 1)
                route.append((e * domains + d, place[0] * domains + place[1]))
        return lax.ppermute(x, ("energy", "domain"), route)

    def across(x, k):
        return lax.ppermute(x, "energy", [(e, e ^ k) for e in range(energies)])

    held_retarded, held_coupling, held_less, held_great, *less_set = kernel_call(
        functools.partial(first_kernel, blocks),
        [series(blocks)] * 4 + [series(blocks - 1), series(blocks), block],
        in_place(retarded, coupling, sigma_lesser, sigma_greater),
        (5 * blocks - 3) * unit,
        in_specs=[HBM] * 4,
        scratch=[pltpu.SemaphoreType.DMA((4 * blocks, 2))],
    )
    early_less = less_set[2]
    lower_less = swap(early_less)
    later_steps, less_sources, less_total, *great_set = kernel_call(
        functools.partial(second_kernel, blocks),
        [series(blocks - 1), series(blocks), block]
        + [block, series(blocks), block, block],
        (held_retarded, held_coupling, held_less, held_great, *less_set),
        (5 * blocks - 2) * unit,
        aliases={4: 0, 5: 1},
    )
    early_great, early_whole = great_set[2:]
    (joined_less,) = kernel_call(
        join_first_kernel, [block], (lower_less, early_whole, early_less), 2 * unit
    )
    lower_less = swap(less_total)
    lower_great = swap(early_great)
    first_step, great_sources, great_total, whole = kernel_call(
        functools.partial(third_kernel, blocks),
        [block, series(blocks), block, block],
        (held_retarded, held_coupling, held_great, later_steps, *great_set),
        (5 * blocks - 2) * unit,
        aliases={4: 0, 5: 1},
    )
    (joined_great,) = kernel_call(
        join_first_kernel, [block], (lower_great, early_whole, early_great), 2 * unit
    )
    lower_great = swap(great_total)
    lower_whole = swap(whole)
    (chip_less,) = kernel_call(
        join_kernel, [block], (joined_less, lower_less, whole, less_total), 2 * unit
    )
    (chip_whole,) = kernel_call(join_whole_kernel, [block], (whole, lower_whole), unit)
    (chip_great,) = kernel_call(
        join_kernel, [block], (joined_great, lower_great, whole, great_total), 2 * unit
    )
    given, own_parts, shifts = kernel_call(
        functools.partial(prepare_kernel, blocks, energies, chosen),
        [
            jax.ShapeDtypeStruct(
                (energies * (rows + half) + pl.cdiv(energies, 2) * rows, 2 * order), BF16
            ),
            jax.ShapeDtypeStruct((energies * rows, order), BF16),
            jax.ShapeDtypeStruct((energies, 8, half), jnp.int32),
        ],
        (
            *in_place(tiles, offsets),
            first_step,
            later_steps,
            less_sources,
            lower_less,
            less_total,
            chip_less,
            great_sources,
            lower_great,
            great_total,
            chip_great,
            lower_whole,
            whole,
            chip_whole,
        ),
        5 * unit,
        in_specs=[HBM] * 2 + [VMEM] * 13,
        scratch=[pltpu.VMEM((blocks, order, 2 * order), BF16)] * 3
        + [
            pltpu.SMEM(tiles.shape, jnp.int32),
            pltpu.SMEM(offsets.shape, jnp.int32),
            pltpu.SemaphoreType.DMA((2,)),
        ],
    )

    taken = swap(given)

    def step_on(z, state, kept, source):
        return kernel_call(
            functools.partial(advance_kernel, z),
            [block, block],
            (state, chip_whole, source, *kept),
            2 * unit,
        )

    less, great = joined_less, joined_great
    less_in, great_in = (), ()
    for z in range(1, chips):
        less = hop(less, z, lower=z == chips - 1)
        great = hop(great, z)
        if z < chips - 1:
            less, *less_in = step_on(z, less, less_in, chip_less)
            great, *great_in = step_on(z, great, great_in, chip_great)
    if not less_in:
        less_in, great_in = [jnp.zeros_like(less)], [jnp.zeros_like(great)]
    near, kept = swap(*less_in), great_in[0]
    shared = (given, taken, own_parts)
    double = pltpu.VMEM((2 * order, 2 * order), BF16)
    sent = range(1, energies)
    pair = jax.ShapeDtypeStruct((2, rows, order), BF16)
    pieces = ()
    for on_last, arrived in ((False, (near, kept)), (True, (less, great))):
        operands = (*arrived, *shared, *pieces)
        pieces = kernel_call(
            functools.partial(finish_kernel, energies, sent, chips - 1, on_last),
            [pair] * len(sent),
            operands,
            5 * unit,
            scratch=[double],
            aliases={len(operands) - len(pieces) + i: i for i in range(len(pieces))},
        )
    pieces = [across(piece, k) for k, piece in zip(sent, pieces)]
    (own,) = kernel_call(
        functools.partial(finish_own_kernel, energies, chips - 1),
        [pair],
        (near, kept, less, great, *shared),
        2 * unit,
        scratch=[double] + [pltpu.VMEM((order, 2 * order), BF16)] * 2,
    )
    pieces = [own, *pieces]
    (packed,) = kernel_call(
        functools.partial(pack_kernel, energies),
        [jax.ShapeDtypeStruct((energies, rows, order), BF16)],
        pieces,
        0,
    )
    shares = kernel_call(
        functools.partial(convolve_kernel, energies),
        [piece] * energies,
        (shifts, swap(packed), *pieces),
        8 * energies * energies * rows * half,
        scratch=[pltpu.VMEM((energies, rows, order), BF16)] * 2,
    )
    shares = [shares[0]] + [across(shares[k], k) for k in range(1, energies)]
    (result,) = kernel_call(
        functools.partial(gather_kernel, energies),
        [jax.ShapeDtypeStruct((energies, rows, order), BF16)],
        shares,
        0,
        out_specs=[HBM],
        scratch=[pltpu.SemaphoreType.DMA((energies,))],
    )
    return result.reshape(1, blocks, chosen, half, order)


def solution(mesh):
    placed = (
        P("energy", "domain", None, None),
        P("domain", None, None),
        P("energy", "domain", None, None),
        P("energy", "domain", None, None),
        P("domain", None),
        P(),
    )

    return jax.shard_map(
        shards,
        mesh=mesh,
        in_specs=placed,
        out_specs=P("energy", "domain", None, None, None),
        check_vma=False,
    )
```
